256 devices in a mesh: seq: 32 (over z, x), head: 8 (over y, core).
Axes of the slice: x: 4, y: 4, z: 8, core: 2. Of those that a mesh axis runs over, the one named last changes fastest.
Arguments:
- queries: bfloat16 [32768, 8192], P('seq', 'head'), may hold values from -6 to 6
- key_vectors: bfloat16 [32768, 8192], P('seq', 'head'), may hold values from -6 to 6
- value_vectors: bfloat16 [32768, 8192], P('seq', 'head'), may hold values from -6 to 6
- level_weight: float32 [32768, 1024], P('seq', 'head'), may hold values from 0.02 to 1
- gate_values: bfloat16 [32768, 8192], P(('seq', 'head')), may hold values from -6 to 6
- norm_gain: float32 [8192], replicated, may hold values from 0.5 to 1.5
Outputs:
- normed: bfloat16 [32768, 8192], P(('seq', 'head'))
The draws below stay inside these ranges and needn't reach their ends.
All inputs are finite; a program needn't handle non-finite values.
Results may differ from the reference program's by a relative error of at most 0.012.
Values may be sent and summed in bfloat16 or wider, within the bound.
A program may use at most 128 MiB of HBM per device.

```python
import math
import jax
import jax.numpy as jnp
from jax import lax

HEADS = 64
HEAD_DIM = 128
TOK_DEV = 1024
LEVELS = 16
TOKENS = 32768
D = 8192
N_SEQ = 32


def level_of(stream_key, extent, pieces, smallest, top_value):
    def one(dim, parts):
        heights = jax.random.uniform(jax.random.fold_in(jax.random.fold_in(stream_key, 6), dim), (parts,), jnp.float32, smallest / len(pieces), top_value / len(pieces))
        return jnp.repeat(jnp.exp(heights), extent[dim] // parts).reshape((-1,) + (1,) * (len(extent) - dim - 1))

    factor_of = one(*pieces[0])
    for cut in pieces[1:]:
        factor_of = factor_of * one(*cut)
    return factor_of


def gaussian(rng, extent, deviation, limit, pieces=(), kind=jnp.bfloat16):
    entries = jax.random.normal(rng, extent, jnp.float32) * deviation
    if len(pieces) > 0:
        entries = level_of(rng, extent, pieces, -0.22, 0.18) * entries
    return jnp.clip(entries, min=-limit, max=limit).astype(kind)


def setup_inputs(seed: int = 0) -> dict:
    streams_of = jax.random.split(jax.random.key(seed), 7)
    return {
        "queries": gaussian(streams_of[0], (TOKENS, D), 1.0, 6.0, ((0, 32), (1, 8))),
        "key_vectors": gaussian(streams_of[1], (TOKENS, D), 1.0, 6.0, ((0, 32), (1, 8))),
        "value_vectors": gaussian(streams_of[2], (TOKENS, D), 1.0, 6.0, ((0, 32), (1, 8))),
        "level_weight": jnp.clip(jnp.exp(math.log(1.0) - 3.912023 * jax.random.uniform(streams_of[3], (TOKENS, HEADS * LEVELS), jnp.float32) ** level_of(streams_of[3], (TOKENS, HEADS * LEVELS), ((0, 32), (1, 8)), -0.2, 0.2)), 0.02, 1.0),
        "gate_values": gaussian(streams_of[4], (TOKENS, D), 1.0, 6.0, ((0, 256),)),
        "norm_gain": jnp.clip(1.0 + 0.1 * jax.random.normal(streams_of[5], (D,), jnp.float32), 0.5, 1.5),
    }


def bit_levels(count):
    indices = jnp.arange(count, dtype=jnp.int32)
    mixed = jnp.bitwise_xor(indices[:, None], indices[None, :])
    levels = jnp.zeros((count, count), jnp.int32)
    for height in range(count.bit_length() - 1):
        levels = levels + (mixed >= 1 << height).astype(jnp.int32)
    causal = indices[None, :] <= indices[:, None]
    return (levels, causal)

def local_attention(query_head, key_head, value_head, weight_head, levels, causal):
    scores = jnp.dot(query_head, key_head.T, preferred_element_type=jnp.float32)
    factor = jnp.zeros(scores.shape, jnp.float32)
    for height in range(query_head.shape[0].bit_length()):
        factor = factor + jnp.where(levels == height, weight_head[:, height:height + 1], jnp.float32(0.0))
    weighted = jnp.where(causal, scores * factor, jnp.float32(0.0)).astype(jnp.bfloat16)
    return jnp.dot(weighted, value_head, preferred_element_type=jnp.float32)

def reference(queries, key_vectors, value_vectors, level_weight, gate_values, norm_gain):
    width = HEADS * HEAD_DIM
    seq_bits = N_SEQ.bit_length() - 1
    local_bits = TOK_DEV.bit_length() - 1
    query_blocks = queries.reshape(N_SEQ, TOK_DEV, HEADS, HEAD_DIM)
    key_blocks = key_vectors.reshape(N_SEQ, TOK_DEV, HEADS, HEAD_DIM)
    value_blocks = value_vectors.reshape(N_SEQ, TOK_DEV, HEADS, HEAD_DIM)
    weight_blocks = level_weight.reshape(N_SEQ, TOK_DEV, HEADS, LEVELS)

    def state_of(inputs):
        return jnp.einsum('che,chf->hef', inputs[0].astype(jnp.float32), inputs[1].astype(jnp.float32), precision=lax.Precision.HIGHEST)
    states = lax.map(state_of, (key_blocks, value_blocks))
    left_sums = []
    for height in range(1, seq_bits + 1):
        span = 2 ** (height - 1)
        grouped = states.reshape(N_SEQ // (2 * span), 2, span, HEADS, HEAD_DIM, HEAD_DIM)
        left_sums.append(lax.optimization_barrier(jnp.sum(grouped[:, 0], axis=1)))
    levels, causal = bit_levels(TOK_DEV)

    def per_block(inputs):
        query_block, key_block, value_block, weight_block, position = inputs

        def per_head(head_inputs):
            return local_attention(head_inputs[0], head_inputs[1], head_inputs[2], head_inputs[3], levels, causal)
        inner = lax.map(per_head, (query_block.transpose(1, 0, 2), key_block.transpose(1, 0, 2), value_block.transpose(1, 0, 2), weight_block.transpose(1, 0, 2)))
        inner = inner.transpose(1, 0, 2)
        cross = jnp.zeros((TOK_DEV, HEADS, HEAD_DIM), jnp.float32)
        for height in range(1, seq_bits + 1):
            chosen = lax.dynamic_index_in_dim(left_sums[height - 1], jnp.right_shift(position, height).astype(jnp.int32), 0, keepdims=False)
            upper = (jnp.right_shift(position, height - 1) & 1).astype(jnp.float32)
            rounded = (chosen * upper).astype(jnp.bfloat16)
            term = jnp.einsum('che,hef->chf', query_block.astype(jnp.float32), rounded.astype(jnp.float32), precision=lax.Precision.HIGHEST)
            cross = cross + weight_block[:, :, local_bits + height, None] * term
        return (inner + cross).reshape(TOK_DEV, width).astype(jnp.bfloat16)
    attended = lax.map(per_block, (query_blocks, key_blocks, value_blocks, weight_blocks, jnp.arange(N_SEQ, dtype=jnp.int32)))
    attended = attended.reshape(N_SEQ * TOK_DEV, width).astype(jnp.float32)
    mean_square = lax.optimization_barrier(jnp.mean(attended * attended, axis=1, keepdims=True))
    gating = jax.nn.silu(gate_values.astype(jnp.float32))
    return (attended * lax.rsqrt(mean_square + 1e-06) * norm_gain[None, :] * gating).astype(jnp.bfloat16)
```

```python
import functools
import jax
import jax.numpy as jnp
from jax import lax
from jax.experimental import pallas as pl
from jax.experimental.pallas import tpu as pltpu
from jax.sharding import PartitionSpec as P

HEAD_DIM = 128
LEVELS = 16
CHUNK = 128
MESH = pl.DeviceIdType.MESH
F32 = jnp.float32
BF16 = jnp.bfloat16


def partner_masks(n_seq):
    masks = {32: (1, 3, 4, 8, 28)}
    return masks.get(n_seq, tuple(1 << b for b in range(n_seq.bit_length() - 1)))


def kernel(
    n_seq, n_head, q_hbm, k_hbm, v_hbm, w_hbm, gate_hbm, gain_hbm, out_hbm,
    qb, kb, vb, wb, gateb, gainb, gsb, levb, inner, wq, tiers, run, sbuf, loc, att, rows, outb, sumsq,
    q_sem, k_sem, v_sem, w_sem, gate_sem, gain_sem, out_sem,
    xs_sem, xr_sem, as_sem, ar_sem,
):
    masks = partner_masks(n_seq)
    steps = len(masks)
    heads = qb.shape[0]
    count = qb.shape[1]
    chunks = count // CHUNK
    chunk_bits = CHUNK.bit_length() - 1
    local_bits = count.bit_length() - 1
    tokens_out = rows.shape[1]
    me_seq = lax.axis_index("seq")
    me_head = lax.axis_index("head")

    def columns(h):
        return pl.ds(pl.multiple_of(h * HEAD_DIM, HEAD_DIM), HEAD_DIM)

    def load_k(h):
        return pltpu.make_async_copy(k_hbm.at[:, columns(h)], kb.at[h], k_sem.at[h])

    def load_v(h):
        return pltpu.make_async_copy(v_hbm.at[:, columns(h)], vb.at[h], v_sem.at[h])

    def load_q(h):
        return pltpu.make_async_copy(q_hbm.at[:, columns(h)], qb.at[h], q_sem.at[h])

    load_w = pltpu.make_async_copy(w_hbm, wb, w_sem)
    load_gate = pltpu.make_async_copy(gate_hbm, gateb, gate_sem)
    load_gain = pltpu.make_async_copy(gain_hbm, gainb, gain_sem)

    def tier_of(s, h):
        return tiers.at[h, s * HEAD_DIM : (s + 1) * HEAD_DIM, :]

    def exchange(s, h):
        return pltpu.make_async_remote_copy(
            src_ref=sbuf.at[s, h],
            dst_ref=tier_of(s, h),
            send_sem=xs_sem.at[s, h],
            recv_sem=xr_sem.at[s, h],
            device_id={"seq": me_seq ^ masks[s]},
            device_id_type=MESH,
        )

    def tokens_of(j):
        return pl.ds(pl.multiple_of(j * tokens_out, tokens_out), tokens_out)

    def scatter(k, h):
        to = me_head ^ k
        return pltpu.make_async_remote_copy(
            src_ref=att.at[h, tokens_of(to), :],
            dst_ref=rows.at[me_head * heads + h],
            send_sem=as_sem.at[k, h],
            recv_sem=ar_sem.at[k, h],
            device_id={"head": to},
            device_id_type=MESH,
        )

    def keep(h):
        return pltpu.make_async_copy(
            att.at[h, tokens_of(me_head), :], rows.at[me_head * heads + h], as_sem.at[0, h]
        )

    barrier = pltpu.get_barrier_semaphore()
    for mask in masks:
        pl.semaphore_signal(barrier, inc=1, device_id={"seq": me_seq ^ mask}, device_id_type=MESH)
    for k in range(1, n_head):
        pl.semaphore_signal(barrier, inc=1, device_id={"head": me_head ^ k}, device_id_type=MESH)

    @pl.loop(0, heads)
    def _(h):
        load_k(h).start()
        load_v(h).start()

    load_w.start()

    @pl.loop(0, heads)
    def _(h):
        load_q(h).start()

    load_gate.start()
    load_gain.start()

    t_id = lax.broadcasted_iota(jnp.int32, (CHUNK, CHUNK), 0)
    s_id = lax.broadcasted_iota(jnp.int32, (CHUNK, CHUNK), 1)
    mixed = t_id ^ s_id
    level = jnp.zeros((CHUNK, CHUNK), jnp.int32)
    for height in range(chunk_bits):
        level = level + (mixed >= 1 << height).astype(jnp.int32)
    levb[...] = level
    sumsq[...] = jnp.zeros_like(sumsq)

    def part(h, c):
        at = slice(c * CHUNK, (c + 1) * CHUNK)
        return lax.dot_general(
            kb[h, at, :], vb[h, at, :], (((0,), (0,)), ((), ())), preferred_element_type=F32
        )

    def span_sum(h, first, size):
        if size == 1:
            return part(h, first)
        half = size // 2
        left = span_sum(h, first, half)
        loc[h, loc_slot(first, half)] = left.astype(BF16)
        return left + span_sum(h, first + half, half)

    def loc_slot(first, half):
        base, size = 0, 1
        while size < half:
            base += chunks // (2 * size)
            size *= 2
        return base + first // (2 * half)

    @pl.loop(0, heads)
    def _(h):
        load_k(h).wait()
        load_v(h).wait()
        total = span_sum(h, 0, chunks)
        run[h] = total
        sbuf[0, h] = total.astype(BF16)

        @pl.when(h == 0)
        def _():
            pl.semaphore_wait(barrier, steps + n_head - 1)

        exchange(0, h).start()

    load_w.wait()
    slot = lax.broadcasted_iota(jnp.int32, (1, wb.shape[1]), 1) & (LEVELS - 1)
    taken = jnp.ones((1, wb.shape[1]), F32)
    for s in range(steps):
        bit = (lax.shift_right_logical(me_seq, s) & 1).astype(F32)
        taken = jnp.where(slot == local_bits + 1 + s, bit, taken)
    wb[...] = wb[...] * taken

    def inside(h):
        load_q(h).wait()
        pick = levb[...] + h * LEVELS
        causal = lax.broadcasted_iota(jnp.int32, (CHUNK, CHUNK), 1) <= lax.broadcasted_iota(
            jnp.int32, (CHUNK, CHUNK), 0
        )
        for c in range(chunks):
            at = slice(c * CHUNK, (c + 1) * CHUNK)
            q_c = qb[h, at, :]
            w_c = wb[at, :]
            q_f = q_c.astype(F32)

            def weighted_q(lev):
                w_l = jnp.take_along_axis(
                    w_c, jnp.full((CHUNK, CHUNK), h * LEVELS + lev, jnp.int32), axis=1
                )
                return (q_f * w_l).astype(BF16)

            scores = lax.dot_general(
                q_c, kb[h, at, :], (((1,), (1,)), ((), ())), preferred_element_type=F32
            )
            factor = jnp.take_along_axis(w_c, pick, axis=1)
            left = [jnp.where(causal, scores * factor, F32(0.0)).astype(BF16)]
            right = [vb[h, at, :]]
            for b in range(chunks.bit_length() - 1):
                if c >> b & 1:
                    left.append(weighted_q(chunk_bits + 1 + b))
                    right.append(loc[h, loc_slot((c >> b << b) - (1 << b), 1 << b)])
            inner[h, at, :] = jnp.dot(
                jnp.concatenate(left, axis=1),
                jnp.concatenate(right, axis=0),
                preferred_element_type=F32,
            )
            for s in range(steps):
                wq[h, at, s * HEAD_DIM : (s + 1) * HEAD_DIM] = weighted_q(local_bits + 1 + s)

    def service(s, h):
        exchange(s, h).wait_recv()
        if s < steps - 1:
            total = run[h] + tier_of(s, h)[...].astype(F32)
            run[h] = total
            sbuf[s + 1, h] = total.astype(BF16)
            exchange(s + 1, h).start()
            return
        cross = jnp.dot(wq[h], tiers[h], preferred_element_type=F32)
        att[h] = (inner[h] + cross).astype(BF16)
        for k in range(1, n_head):
            scatter(k, h).start()
        keep(h).start()

    lag = 2

    @pl.loop(0, heads + lag * (steps - 1) + 1)
    def _(i):
        @pl.when(i < heads)
        def _():
            inside(jnp.minimum(i, heads - 1))

        for s in range(steps):
            h = i - 1 - lag * s if s < steps - 1 else i - lag * s - 1

            @pl.when((h >= 0) & (h < heads))
            def _(s=s, h=h):
                service(s, h)

    load_gate.wait()
    load_gain.wait()

    wide = n_head * HEAD_DIM

    @pl.loop(0, heads)
    def _(h):
        at = pl.ds(pl.multiple_of(h * wide, wide), wide)
        gate = gateb[:, at].astype(F32)
        gsb[:, at] = gainb[:, at] * (gate / (1.0 + jnp.exp(-gate)))
        keep(h).wait()
        for k in range(1, n_head):
            scatter(k, h).wait_recv()
        total = sumsq[...]
        for j in range(n_head):
            x = rows[j * heads + h].astype(F32)
            total = total + x * x
        sumsq[...] = total

    mean_square = jnp.sum(sumsq[...], axis=1, keepdims=True) * (1.0 / (heads * n_head * HEAD_DIM))
    scale = jnp.broadcast_to(lax.rsqrt(mean_square + 1e-06), (tokens_out, HEAD_DIM))
    sumsq[...] = scale

    def store(j):
        span = heads * HEAD_DIM
        return pltpu.make_async_copy(
            outb.at[j], out_hbm.at[:, pl.ds(pl.multiple_of(j * span, span), span)], out_sem.at[j]
        )

    @pl.loop(0, n_head)
    def _(j):
        for u in range(heads):
            at = pl.ds(pl.multiple_of((j * heads + u) * HEAD_DIM, HEAD_DIM), HEAD_DIM)
            x = rows[j * heads + u].astype(F32)
            outb[j, :, u * HEAD_DIM : (u + 1) * HEAD_DIM] = (x * sumsq[...] * gsb[:, at]).astype(BF16)
        store(j).start()

    @pl.loop(0, n_head)
    def _(j):
        store(j).wait()

    @pl.loop(0, heads)
    def _(h):
        for s in range(steps):
            exchange(s, h).wait_send()
        for k in range(1, n_head):
            scatter(k, h).wait_send()


def per_device(queries, key_vectors, value_vectors, level_weight, gate_values, norm_gain):
    count, features = queries.shape
    heads = features // HEAD_DIM
    n_seq, n_head = lax.axis_size("seq"), lax.axis_size("head")
    steps = n_seq.bit_length() - 1
    tokens_out, width = gate_values.shape
    chunks = count // CHUNK
    vmem, dma = pltpu.VMEM, pltpu.SemaphoreType.DMA
    return pl.pallas_call(
        functools.partial(kernel, n_seq, n_head),
        out_shape=jax.ShapeDtypeStruct((tokens_out, width), BF16),
        in_specs=[pl.BlockSpec(memory_space=pl.ANY)] * 6,
        out_specs=pl.BlockSpec(memory_space=pl.ANY),
        scratch_shapes=[
            vmem((heads, count, HEAD_DIM), BF16),
            vmem((heads, count, HEAD_DIM), BF16),
            vmem((heads, count, HEAD_DIM), BF16),
            vmem((count, heads * LEVELS), F32),
            vmem((tokens_out, width), BF16),
            vmem((1, width), F32),
            vmem((tokens_out, width), F32),
            vmem((CHUNK, CHUNK), jnp.int32),
            vmem((heads, count, HEAD_DIM), F32),
            vmem((heads, count, steps * HEAD_DIM), BF16),
            vmem((heads, steps * HEAD_DIM, HEAD_DIM), BF16),
            vmem((heads, HEAD_DIM, HEAD_DIM), F32),
            vmem((steps, heads, HEAD_DIM, HEAD_DIM), BF16),
            vmem((heads, chunks - 1, HEAD_DIM, HEAD_DIM), BF16),
            vmem((heads, count, HEAD_DIM), BF16),
            vmem((n_head * heads, tokens_out, HEAD_DIM), BF16),
            vmem((n_head, tokens_out, heads * HEAD_DIM), BF16),
            vmem((tokens_out, HEAD_DIM), F32),
            dma((heads,)),
            dma((heads,)),
            dma((heads,)),
            dma,
            dma,
            dma,
            dma((n_head,)),
            dma((steps, heads)),
            dma((steps, heads)),
            dma((n_head, heads)),
            dma((n_head, heads)),
        ],
        compiler_params=pltpu.CompilerParams(
            collective_id=0, has_side_effects=True, vmem_limit_bytes=60 << 20
        ),
    )(queries, key_vectors, value_vectors, level_weight, gate_values, norm_gain[None, :])


def solution(mesh):
    placed = (
        P("seq", "head"),
        P("seq", "head"),
        P("seq", "head"),
        P("seq", "head"),
        P(("seq", "head"), None),
        P(),
    )
    return jax.shard_map(
        per_device, mesh=mesh, in_specs=placed, out_specs=P(("seq", "head"), None), check_vma=False
    )
```

```python
import functools
import jax
import jax.numpy as jnp
from jax import lax
from jax.experimental import pallas as pl
from jax.experimental.pallas import tpu as pltpu
from jax.sharding import PartitionSpec as P

HEAD_DIM = 128
LEVELS = 16
CHUNK = 128
MESH = pl.DeviceIdType.MESH
F32 = jnp.float32
BF16 = jnp.bfloat16


PLAN = ((1, 2, 3), (4, 8, 12), (28, 24))
PARTS = 2
DUE = ((1, 2), (6, 3), (11, 4))
FAR_FIRST = (4, 5, 2, 3, 6, 7, 1)


def kernel(
    n_seq, n_head, q_hbm, k_hbm, v_hbm, w_hbm, gate_hbm, gain_hbm, out_ref,
    qb, kb, vb, wb, wlow, spread, gateb, gainb, gsb, levb, inner, wq, tiers, xbuf, run, sbuf, loc, att, rows, sumsq,
    q_sem, k_sem, v_sem, w_sem, gate_sem, gain_sem,
    xs_sem, xr_sem, ready, ys_sem, yr_sem, keep_sem,
):
    plan = PLAN
    steps = len(plan)
    levels_out = n_seq.bit_length() - 1
    heads = qb.shape[0]
    count = qb.shape[1]
    chunks = count // CHUNK
    chunk_bits = CHUNK.bit_length() - 1
    local_bits = count.bit_length() - 1
    tokens_out = sumsq.shape[0]
    me_seq = lax.axis_index("seq")
    me_head = lax.axis_index("head")

    def columns(h):
        return pl.ds(pl.multiple_of(h * HEAD_DIM, HEAD_DIM), HEAD_DIM)

    def load_k(h):
        return pltpu.make_async_copy(k_hbm.at[:, columns(h)], kb.at[h], k_sem.at[h])

    def load_v(h):
        return pltpu.make_async_copy(v_hbm.at[:, columns(h)], vb.at[h], v_sem.at[h])

    def load_q(h):
        return pltpu.make_async_copy(q_hbm.at[:, columns(h)], qb.at[h], q_sem.at[h])

    load_w = pltpu.make_async_copy(w_hbm, wb, w_sem)
    load_gate = pltpu.make_async_copy(gate_hbm, gateb, gate_sem)
    load_gain = pltpu.make_async_copy(gain_hbm, gainb, gain_sem)

    def tier_of(m, h):
        return tiers.at[h, m * HEAD_DIM : (m + 1) * HEAD_DIM, :]

    def landing(s, j, h):
        return tier_of(2 * s, h) if j == 0 or s == 2 else xbuf.at[2 * s + j - 1, h]

    me_z = lax.shift_right_logical(me_seq, 2)
    in_four = me_z & 3
    upper = me_z >= 4

    def upward(j):
        return (in_four ^ (j + 1)) > in_four

    def downward(j):
        return (me_z ^ (j + 1)) == 0

    def sends(s, j):
        if s == 1:
            return upward(j) | downward(j)
        return (me_z == 0) | (me_z == 3)

    def receives(s, j):
        if s == 1:
            return ((in_four ^ (j + 1)) < in_four) | (me_z == 0)
        near = (me_z == 4) | (me_z == 7) if j == 0 else (me_z == 5) | (me_z == 6)
        return near

    def start_exchange(s, j, h):
        if s == 0:
            exchange(s, j, h).start()
            return

        @pl.when(sends(s, j))
        def _():
            if s == 1:
                @pl.when((h == 0) & upward(j))
                def _():
                    pl.semaphore_wait(ready.at[j], 1)
            else:
                @pl.when(h == 0)
                def _():
                    pl.semaphore_wait(ready.at[3 + j], 1)
            exchange(s, j, h).start()

    def wait_exchange(s, j, h):
        if s == 0:
            exchange(s, j, h).wait_recv()
            return

        @pl.when(receives(s, j))
        def _():
            exchange(s, j, h).wait_recv()

    def row_partner(mask):
        return {"seq": me_seq ^ mask}

    def exchange(s, j, h):
        n = sum(len(p) for p in plan[:s]) + j
        return pltpu.make_async_remote_copy(
            src_ref=sbuf.at[s, h],
            dst_ref=landing(s, j, h),
            send_sem=xs_sem.at[n, h],
            recv_sem=xr_sem.at[n, h],
            device_id={"seq": me_seq ^ plan[s][j]},
            device_id_type=MESH,
        )

    def tokens_of(j):
        return pl.ds(pl.multiple_of(j * tokens_out, tokens_out), tokens_out)

    def scatter(k, h):
        return pltpu.make_async_remote_copy(
            src_ref=att.at[h, tokens_of(me_head ^ k), :],
            dst_ref=rows.at[me_head, h],
            send_sem=ys_sem.at[k, h],
            recv_sem=yr_sem.at[k, h],
            device_id={"head": me_head ^ k},
            device_id_type=MESH,
        )

    def keep(h):
        return pltpu.make_async_copy(att.at[h, tokens_of(me_head), :], rows.at[me_head, h], keep_sem.at[h])

    load_k(0).start()
    load_v(0).start()
    barrier = pltpu.get_barrier_semaphore()
    for mask in plan[0]:
        pl.semaphore_signal(barrier, inc=1, device_id=row_partner(mask), device_id_type=MESH)
    for k in range(1, n_head):
        pl.semaphore_signal(barrier, inc=1, device_id={"head": me_head ^ k}, device_id_type=MESH)

    for j, mask in enumerate(plan[1]):
        @pl.when(upward(j))
        def _(mask=mask):
            pl.semaphore_signal(barrier, inc=1, device_id=row_partner(mask), device_id_type=MESH)

    for j, mask in enumerate(plan[2]):
        @pl.when(sends(2, j))
        def _(mask=mask):
            pl.semaphore_signal(barrier, inc=1, device_id=row_partner(mask), device_id_type=MESH)

    @pl.loop(1, heads)
    def _(h):
        load_k(h).start()
        load_v(h).start()

    load_w.start()

    @pl.loop(0, heads)
    def _(h):
        load_q(h).start()

    load_gate.start()
    load_gain.start()

    t_id = lax.broadcasted_iota(jnp.int32, (CHUNK, CHUNK), 0)
    s_id = lax.broadcasted_iota(jnp.int32, (CHUNK, CHUNK), 1)
    mixed = t_id ^ s_id
    level = jnp.zeros((CHUNK, CHUNK), jnp.int32)
    for height in range(chunk_bits):
        level = level + (mixed >= 1 << height).astype(jnp.int32)
    levb[...] = level
    sumsq[...] = jnp.zeros_like(sumsq)

    @pl.loop(0, heads)
    def _(h):
        for s in (1, 2):
            for j in range(len(plan[s])):
                if s == 2 and j == 1:
                    continue
                empty = jnp.logical_not(receives(s, j)) if s == 1 else jnp.logical_not(upper)

                @pl.when(empty)
                def _(s=s, j=j):
                    landing(s, j, h)[...] = jnp.zeros((HEAD_DIM, HEAD_DIM), BF16)

    @pl.loop(0, heads)
    def _(h):
        row = lax.broadcasted_iota(jnp.int32, (spread.shape[1], HEAD_DIM), 0)
        for n in range(spread.shape[2] // HEAD_DIM):
            here = row == h * LEVELS + chunk_bits + 1 + n
            spread[h, :, n * HEAD_DIM : (n + 1) * HEAD_DIM] = jnp.where(here, F32(1.0), F32(0.0)).astype(BF16)

    def part(h, c):
        at = slice(c * CHUNK, (c + 1) * CHUNK)
        return lax.dot_general(
            kb[h, at, :], vb[h, at, :], (((0,), (0,)), ((), ())), preferred_element_type=F32
        )

    def loc_slot(first, half):
        base, size = 0, 1
        while size < half:
            base += chunks // (2 * size)
            size *= 2
        return base + first // (2 * half)

    def span_sum(h, first, size):
        if size == 1:
            return part(h, first)
        half = size // 2
        left = span_sum(h, first, half)
        loc[h, loc_slot(first, half)] = left.astype(BF16)
        return left + span_sum(h, first + half, half)

    @pl.loop(0, heads)
    def _(h):
        load_k(h).wait()
        load_v(h).wait()
        total = span_sum(h, 0, chunks)
        run[h] = total
        sbuf[0, h] = total.astype(BF16)

        @pl.when(h == 0)
        def _():
            pl.semaphore_wait(
                barrier, len(plan[0]) + n_head - 1 + in_four + jnp.where(upper, 1, 0)
            )
            for j, mask in enumerate(plan[1]):
                @pl.when((in_four ^ (j + 1)) < in_four)
                def _(j=j, mask=mask):
                    pl.semaphore_signal(
                        ready.at[j], inc=1, device_id=row_partner(mask), device_id_type=MESH
                    )

            for j, mask in enumerate(plan[2]):
                @pl.when(receives(2, j))
                def _(j=j, mask=mask):
                    pl.semaphore_signal(
                        ready.at[3 + j], inc=1, device_id=row_partner(mask), device_id_type=MESH
                    )

        for j in range(len(plan[0])):
            start_exchange(0, j, h)

    load_w.wait()
    slot = lax.broadcasted_iota(jnp.int32, (1, wb.shape[1]), 1) & (LEVELS - 1)
    taken = jnp.ones((1, wb.shape[1]), F32)
    for m in range(levels_out):
        bit = (lax.shift_right_logical(me_seq, m) & 1).astype(F32)
        taken = jnp.where(slot == local_bits + 1 + m, bit, taken)
    wlow[...] = (wb[...] * taken).astype(BF16)

    def inside(h, which):
        pick = levb[...] + h * LEVELS
        causal = lax.broadcasted_iota(jnp.int32, (CHUNK, CHUNK), 1) <= lax.broadcasted_iota(
            jnp.int32, (CHUNK, CHUNK), 0
        )
        which = list(which)
        base = which[0] * CHUNK
        span = slice(base, base + len(which) * CHUNK)
        inner_bits = chunks.bit_length() - 1

        def weighted_q(n, size, rows_at):
            spread_w = jnp.dot(
                wlow[rows_at, :],
                spread[h, :, n * HEAD_DIM : (n + size) * HEAD_DIM],
                preferred_element_type=F32,
            ).astype(BF16)
            q_rows = qb[h, rows_at, :]
            return [q_rows * spread_w[:, m * HEAD_DIM : (m + 1) * HEAD_DIM] for m in range(size)]

        scores = []
        for c in which:
            at = slice(c * CHUNK, (c + 1) * CHUNK)
            scores.append(
                lax.dot_general(
                    qb[h, at, :], kb[h, at, :], (((1,), (1,)), ((), ())), preferred_element_type=F32
                )
            )
        for n in range(0, levels_out, 2):
            size = min(2, levels_out - n)
            for m, scaled in enumerate(weighted_q(inner_bits + n, size, span)):
                wq[h, span, (n + m) * HEAD_DIM : (n + m + 1) * HEAD_DIM] = scaled
        lefts = []
        for c, score in zip(which, scores):
            at = slice(c * CHUNK, (c + 1) * CHUNK)
            factor = jnp.take_along_axis(wb[at, :], pick, axis=1)
            left = [jnp.where(causal, score * factor, F32(0.0)).astype(BF16)]
            bits = [n for n in range(inner_bits) if c >> n & 1]
            if bits == [0, 1]:
                left += weighted_q(0, 2, at)
            else:
                for n in bits:
                    left += weighted_q(n, 1, at)
            lefts.append((c, bits, left))
        for c, bits, left in lefts:
            at = slice(c * CHUNK, (c + 1) * CHUNK)
            right = [vb[h, at, :]] + [
                loc[h, loc_slot((c >> n << n) - (1 << n), 1 << n)] for n in bits
            ]
            inner[h, at, :] = jnp.dot(
                jnp.concatenate(left, axis=1),
                jnp.concatenate(right, axis=0),
                preferred_element_type=F32,
            )

    def service(s, h):
        for j in range(len(plan[s])):
            wait_exchange(s, j, h)
        pair = None
        if len(plan[s]) == 3:
            pair = xbuf[2 * s, h].astype(F32) + xbuf[2 * s + 1, h].astype(F32)
            tier_of(2 * s + 1, h)[...] = pair.astype(BF16)
        if s < steps - 1:
            total = run[h] + tier_of(2 * s, h)[...].astype(F32)
            if pair is not None:
                total = total + pair
            run[h] = total
            sbuf[s + 1, h] = total.astype(BF16)
            for j in range(len(plan[s + 1])):
                start_exchange(s + 1, j, h)
            return
        cross = jnp.dot(wq[h], tiers[h], preferred_element_type=F32)
        att[h] = (inner[h] + cross).astype(BF16)
        for k in FAR_FIRST:
            scatter(k, h).start()
        keep(h).start()

    wide = n_head * HEAD_DIM

    def gating(j):
        at = pl.ds(pl.multiple_of(j * wide, wide), wide)
        gate = gateb[:, at].astype(F32)
        gsb[:, at] = gainb[:, at] * (gate / (1.0 + jnp.exp(-gate)))

    def collect(h):
        keep(h).wait()
        for k in range(1, n_head):
            scatter(k, h).wait_recv()
        total = sumsq[...]
        for j in range(n_head):
            x = rows[j, h].astype(F32)
            total = total + x * x
        sumsq[...] = total

    units = PARTS * heads
    each = chunks // PARTS

    @pl.loop(0, max(units + heads, DUE[-1][0] + DUE[-1][1] * (heads - 1) + 1))
    def _(i):
        for n, (first, rate) in enumerate(DUE):
            h = (i - first) // rate

            @pl.when((i >= first) & (h < heads) & (lax.rem(i - first, rate) == 0))
            def _(n=n, h=h):
                service(n, h)

        for p in range(PARTS):
            @pl.when((i < units) & (lax.rem(i, PARTS) == p))
            def _(p=p):
                h = i // PARTS
                if p == 0:
                    load_q(h).wait()
                inside(h, range(p * each, (p + 1) * each))

        @pl.when(i == units)
        def _():
            load_gate.wait()
            load_gain.wait()

        @pl.when((i >= units) & (i < units + heads))
        def _():
            gating(i - units)

    @pl.loop(0, heads)
    def _(h):
        collect(h)

    mean_square = jnp.sum(sumsq[...], axis=1, keepdims=True) * (1.0 / (heads * n_head * HEAD_DIM))
    scale = jnp.broadcast_to(lax.rsqrt(mean_square + 1e-06), (tokens_out, HEAD_DIM))
    sumsq[...] = scale

    @pl.loop(0, n_head)
    def _(j):
        for h in range(heads):
            at = columns(j * heads + h)
            x = rows[j, h].astype(F32)
            out_ref[:, at] = (x * sumsq[...] * gsb[:, at]).astype(BF16)

    @pl.loop(0, heads)
    def _(h):
        for s in range(steps):
            for j in range(len(plan[s])):
                if s == 0:
                    exchange(s, j, h).wait_send()
                else:
                    @pl.when(sends(s, j))
                    def _(s=s, j=j):
                        exchange(s, j, h).wait_send()

        for k in range(1, n_head):
            scatter(k, h).wait_send()


def per_device(queries, key_vectors, value_vectors, level_weight, gate_values, norm_gain):
    count, features = queries.shape
    heads = features // HEAD_DIM
    n_seq, n_head = lax.axis_size("seq"), lax.axis_size("head")
    levels_out = n_seq.bit_length() - 1
    sends = sum(len(part) for part in PLAN)
    tokens_out, width = gate_values.shape
    chunks = count // CHUNK
    vmem, dma = pltpu.VMEM, pltpu.SemaphoreType.DMA
    return pl.pallas_call(
        functools.partial(kernel, n_seq, n_head),
        out_shape=pltpu.VMEM((tokens_out, width), BF16),
        in_specs=[pl.BlockSpec(memory_space=pl.ANY)] * 6,
        out_specs=pl.BlockSpec(memory_space=pltpu.VMEM),
        scratch_shapes=[
            vmem((heads, count, HEAD_DIM), BF16),
            vmem((heads, count, HEAD_DIM), BF16),
            vmem((heads, count, HEAD_DIM), BF16),
            vmem((count, heads * LEVELS), F32),
            vmem((count, heads * LEVELS), BF16),
            vmem((heads, heads * LEVELS, (chunks.bit_length() - 1 + levels_out) * HEAD_DIM), BF16),
            vmem((tokens_out, width), BF16),
            vmem((1, width), F32),
            vmem((tokens_out, width), F32),
            vmem((CHUNK, CHUNK), jnp.int32),
            vmem((heads, count, HEAD_DIM), F32),
            vmem((heads, count, levels_out * HEAD_DIM), BF16),
            vmem((heads, levels_out * HEAD_DIM, HEAD_DIM), BF16),
            vmem((4, heads, HEAD_DIM, HEAD_DIM), BF16),
            vmem((heads, HEAD_DIM, HEAD_DIM), F32),
            vmem((len(PLAN), heads, HEAD_DIM, HEAD_DIM), BF16),
            vmem((heads, chunks - 1, HEAD_DIM, HEAD_DIM), BF16),
            vmem((heads, count, HEAD_DIM), BF16),
            vmem((n_head, heads, tokens_out, HEAD_DIM), BF16),
            vmem((tokens_out, HEAD_DIM), F32),
            dma((heads,)),
            dma((heads,)),
            dma((heads,)),
            dma,
            dma,
            dma,
            dma((sends, heads)),
            dma((sends, heads)),
            pltpu.SemaphoreType.REGULAR((5,)),
            dma((n_head, heads)),
            dma((n_head, heads)),
            dma((heads,)),
        ],
        compiler_params=pltpu.CompilerParams(
            collective_id=0, has_side_effects=True, vmem_limit_bytes=58 << 20
        ),
    )(queries, key_vectors, value_vectors, level_weight, gate_values, norm_gain[None, :])


def solution(mesh):
    placed = (
        P("seq", "head"),
        P("seq", "head"),
        P("seq", "head"),
        P("seq", "head"),
        P(("seq", "head"), None),
        P(),
    )
    return jax.shard_map(
        per_device, mesh=mesh, in_specs=placed, out_specs=P(("seq", "head"), None), check_vma=False
    )
```

```python
import functools
import jax
import jax.numpy as jnp
from jax import lax
from jax.experimental import pallas as pl
from jax.experimental.pallas import tpu as pltpu
from jax.sharding import PartitionSpec as P

HEAD_DIM = 128
LEVELS = 16
CHUNK = 128
MESH = pl.DeviceIdType.MESH
F32 = jnp.float32
BF16 = jnp.bfloat16


PLAN = ((1, 2, 3), (4, 8, 12), (28, 24))
PARTS = 2
DUE = ((4, 2), (8, 3), (12, 3))
STATE_DUE = (1, 2)
ROW0_LATER = 2
FAR_FIRST = (4, 5, 2, 3, 6, 7, 1)


def kernel(
    n_seq, n_head, q_hbm, k_hbm, v_hbm, w_hbm, gate_hbm, gain_hbm, out_ref,
    qb, kb, vb, wb, wlow, spread, gateb, gainb, gsb, levb, inner, wq, tiers, xbuf, run, sbuf, loc, att, rows, sumsq,
    q_sem, k_sem, v_sem, w_sem, gate_sem, gain_sem,
    xs_sem, xr_sem, ready, ys_sem, yr_sem, keep_sem,
):
    plan = PLAN
    steps = len(plan)
    levels_out = n_seq.bit_length() - 1
    heads = qb.shape[0]
    count = qb.shape[1]
    chunks = count // CHUNK
    chunk_bits = CHUNK.bit_length() - 1
    local_bits = count.bit_length() - 1
    tokens_out = sumsq.shape[0]
    me_seq = lax.axis_index("seq")
    me_head = lax.axis_index("head")

    def columns(h):
        return pl.ds(pl.multiple_of(h * HEAD_DIM, HEAD_DIM), HEAD_DIM)

    def load_k(h):
        return pltpu.make_async_copy(k_hbm.at[:, columns(h)], kb.at[h], k_sem.at[h])

    def load_v(h):
        return pltpu.make_async_copy(v_hbm.at[:, columns(h)], vb.at[h], v_sem.at[h])

    def load_q(h):
        return pltpu.make_async_copy(q_hbm.at[:, columns(h)], qb.at[h], q_sem.at[h])

    load_w = pltpu.make_async_copy(w_hbm, wb, w_sem)
    load_gate = pltpu.make_async_copy(gate_hbm, gateb, gate_sem)
    load_gain = pltpu.make_async_copy(gain_hbm, gainb, gain_sem)

    def tier_of(m, h):
        return tiers.at[h, m * HEAD_DIM : (m + 1) * HEAD_DIM, :]

    def landing(s, j, h):
        if s == 1:
            return xbuf.at[2 + j, h]
        return tier_of(2 * s, h) if j == 0 or s == 2 else xbuf.at[j - 1, h]

    me_z = lax.shift_right_logical(me_seq, 2)
    in_four = me_z & 3
    upper = me_z >= 4

    def upward(j):
        return (in_four ^ (j + 1)) > in_four

    def downward(j):
        return (me_z ^ (j + 1)) == 0

    def sends(s, j):
        if s == 1:
            return upward(j) | downward(j)
        return (me_z == 0) | (me_z == 3)

    def receives(s, j):
        if s == 1:
            return ((in_four ^ (j + 1)) < in_four) | (me_z == 0)
        near = (me_z == 4) | (me_z == 7) if j == 0 else (me_z == 5) | (me_z == 6)
        return near

    def start_exchange(s, j, h):
        if s == 0:
            exchange(s, j, h).start()
            return

        @pl.when(sends(s, j))
        def _():
            if s == 1:
                @pl.when((h == 0) & upward(j))
                def _():
                    pl.semaphore_wait(ready.at[j], 1)
            else:
                @pl.when(h == 0)
                def _():
                    pl.semaphore_wait(ready.at[3 + j], 1)
            exchange(s, j, h).start()

    def wait_exchange(s, j, h):
        if s == 0:
            exchange(s, j, h).wait_recv()
            return

        @pl.when(receives(s, j))
        def _():
            exchange(s, j, h).wait_recv()

    def row_partner(mask):
        return {"seq": me_seq ^ mask}

    def exchange(s, j, h):
        n = sum(len(p) for p in plan[:s]) + j
        return pltpu.make_async_remote_copy(
            src_ref=sbuf.at[s, h],
            dst_ref=landing(s, j, h),
            send_sem=xs_sem.at[n, h],
            recv_sem=xr_sem.at[n, h],
            device_id={"seq": me_seq ^ plan[s][j]},
            device_id_type=MESH,
        )

    def tokens_of(j):
        return pl.ds(pl.multiple_of(j * tokens_out, tokens_out), tokens_out)

    def scatter(k, h):
        return pltpu.make_async_remote_copy(
            src_ref=att.at[h, tokens_of(me_head ^ k), :],
            dst_ref=rows.at[me_head, h],
            send_sem=ys_sem.at[k, h],
            recv_sem=yr_sem.at[k, h],
            device_id={"head": me_head ^ k},
            device_id_type=MESH,
        )

    def keep(h):
        return pltpu.make_async_copy(att.at[h, tokens_of(me_head), :], rows.at[me_head, h], keep_sem.at[h])

    load_k(0).start()
    load_v(0).start()
    barrier = pltpu.get_barrier_semaphore()
    for mask in plan[0]:
        pl.semaphore_signal(barrier, inc=1, device_id=row_partner(mask), device_id_type=MESH)
    for k in range(1, n_head):
        pl.semaphore_signal(barrier, inc=1, device_id={"head": me_head ^ k}, device_id_type=MESH)

    for j, mask in enumerate(plan[1]):
        @pl.when(upward(j))
        def _(mask=mask):
            pl.semaphore_signal(barrier, inc=1, device_id=row_partner(mask), device_id_type=MESH)

    for j, mask in enumerate(plan[2]):
        @pl.when(sends(2, j))
        def _(mask=mask):
            pl.semaphore_signal(barrier, inc=1, device_id=row_partner(mask), device_id_type=MESH)

    @pl.loop(1, heads)
    def _(h):
        load_k(h).start()
        load_v(h).start()

    load_w.start()

    @pl.loop(0, heads)
    def _(h):
        load_q(h).start()

    load_gate.start()
    load_gain.start()

    t_id = lax.broadcasted_iota(jnp.int32, (CHUNK, CHUNK), 0)
    s_id = lax.broadcasted_iota(jnp.int32, (CHUNK, CHUNK), 1)
    mixed = t_id ^ s_id
    level = jnp.zeros((CHUNK, CHUNK), jnp.int32)
    for height in range(chunk_bits):
        level = level + (mixed >= 1 << height).astype(jnp.int32)
    levb[...] = level
    sumsq[...] = jnp.zeros_like(sumsq)

    @pl.loop(0, heads)
    def _(h):
        for s in (1, 2):
            for j in range(len(plan[s])):
                if s == 2 and j == 1:
                    continue
                empty = jnp.logical_not(receives(s, j)) if s == 1 else jnp.logical_not(upper)

                @pl.when(empty)
                def _(s=s, j=j):
                    landing(s, j, h)[...] = jnp.zeros((HEAD_DIM, HEAD_DIM), BF16)

        @pl.when(me_z == 0)
        def _():
            for m in (2, 3):
                tier_of(m, h)[...] = jnp.zeros((HEAD_DIM, HEAD_DIM), BF16)

    @pl.loop(0, heads)
    def _(h):
        row = lax.broadcasted_iota(jnp.int32, (spread.shape[1], HEAD_DIM), 0)
        for n in range(spread.shape[2] // HEAD_DIM):
            here = row == h * LEVELS + chunk_bits + 1 + n
            spread[h, :, n * HEAD_DIM : (n + 1) * HEAD_DIM] = jnp.where(here, F32(1.0), F32(0.0)).astype(BF16)

    def part(h, c):
        at = slice(c * CHUNK, (c + 1) * CHUNK)
        return lax.dot_general(
            kb[h, at, :], vb[h, at, :], (((0,), (0,)), ((), ())), preferred_element_type=F32
        )

    def loc_slot(first, half):
        base, size = 0, 1
        while size < half:
            base += chunks // (2 * size)
            size *= 2
        return base + first // (2 * half)

    def span_sum(h, first, size):
        if size == 1:
            return part(h, first)
        half = size // 2
        left = span_sum(h, first, half)
        loc[h, loc_slot(first, half)] = left.astype(BF16)
        return left + span_sum(h, first + half, half)

    def state(h):
        load_k(h).wait()
        load_v(h).wait()
        total = span_sum(h, 0, chunks)
        run[h] = total
        sbuf[0, h] = total.astype(BF16)

    def send_state(h):
        for j in range(len(plan[0])):
            start_exchange(0, j, h)

    state(0)
    pl.semaphore_wait(
        barrier, len(plan[0]) + n_head - 1 + in_four + jnp.where(upper, 1, 0)
    )
    for j, mask in enumerate(plan[1]):
        @pl.when((in_four ^ (j + 1)) < in_four)
        def _(j=j, mask=mask):
            pl.semaphore_signal(
                ready.at[j], inc=1, device_id=row_partner(mask), device_id_type=MESH
            )

    for j, mask in enumerate(plan[2]):
        @pl.when(receives(2, j))
        def _(j=j, mask=mask):
            pl.semaphore_signal(
                ready.at[3 + j], inc=1, device_id=row_partner(mask), device_id_type=MESH
            )

    send_state(0)
    load_w.wait()
    slot = lax.broadcasted_iota(jnp.int32, (1, wb.shape[1]), 1) & (LEVELS - 1)
    taken = jnp.ones((1, wb.shape[1]), F32)
    for m in range(levels_out):
        bit = (lax.shift_right_logical(me_seq, m) & 1).astype(F32)
        taken = jnp.where(slot == local_bits + 1 + m, bit, taken)
    wlow[...] = (wb[...] * taken).astype(BF16)

    def inside(h, which):
        pick = levb[...] + h * LEVELS
        causal = lax.broadcasted_iota(jnp.int32, (CHUNK, CHUNK), 1) <= lax.broadcasted_iota(
            jnp.int32, (CHUNK, CHUNK), 0
        )
        which = list(which)
        base = which[0] * CHUNK
        span = slice(base, base + len(which) * CHUNK)
        inner_bits = chunks.bit_length() - 1

        def weighted_q(n, size, rows_at):
            spread_w = jnp.dot(
                wlow[rows_at, :],
                spread[h, :, n * HEAD_DIM : (n + size) * HEAD_DIM],
                preferred_element_type=F32,
            ).astype(BF16)
            q_rows = qb[h, rows_at, :]
            return [q_rows * spread_w[:, m * HEAD_DIM : (m + 1) * HEAD_DIM] for m in range(size)]

        scores = []
        for c in which:
            at = slice(c * CHUNK, (c + 1) * CHUNK)
            scores.append(
                lax.dot_general(
                    qb[h, at, :], kb[h, at, :], (((1,), (1,)), ((), ())), preferred_element_type=F32
                )
            )
        for n in range(0, levels_out, 2):
            size = min(2, levels_out - n)
            for m, scaled in enumerate(weighted_q(inner_bits + n, size, span)):
                wq[h, span, (n + m) * HEAD_DIM : (n + m + 1) * HEAD_DIM] = scaled
        lefts = []
        for c, score in zip(which, scores):
            at = slice(c * CHUNK, (c + 1) * CHUNK)
            factor = jnp.take_along_axis(wb[at, :], pick, axis=1)
            left = [jnp.where(causal, score * factor, F32(0.0)).astype(BF16)]
            bits = [n for n in range(inner_bits) if c >> n & 1]
            if bits == [0, 1]:
                left += weighted_q(0, 2, at)
            else:
                for n in bits:
                    left += weighted_q(n, 1, at)
            lefts.append((c, bits, left))
        for c, bits, left in lefts:
            at = slice(c * CHUNK, (c + 1) * CHUNK)
            right = [vb[h, at, :]] + [
                loc[h, loc_slot((c >> n << n) - (1 << n), 1 << n)] for n in bits
            ]
            inner[h, at, :] = jnp.dot(
                jnp.concatenate(left, axis=1),
                jnp.concatenate(right, axis=0),
                preferred_element_type=F32,
            )

    def service(s, h):
        for j in range(len(plan[s])):
            wait_exchange(s, j, h)
        if s < steps - 1:
            nearest = landing(s, 0, h)[...]
            pair = landing(s, 1, h)[...].astype(F32) + landing(s, 2, h)[...].astype(F32)
            if s == 0:
                tier_of(1, h)[...] = pair.astype(BF16)
            else:
                @pl.when(me_z != 0)
                def _():
                    tier_of(2, h)[...] = nearest
                    tier_of(3, h)[...] = pair.astype(BF16)

            total = run[h] + nearest.astype(F32) + pair
            run[h] = total
            sbuf[s + 1, h] = total.astype(BF16)
            for j in range(len(plan[s + 1])):
                start_exchange(s + 1, j, h)
            return
        cross = jnp.dot(wq[h], tiers[h], preferred_element_type=F32)
        att[h] = (inner[h] + cross).astype(BF16)
        for k in FAR_FIRST:
            scatter(k, h).start()
        keep(h).start()

    wide = n_head * HEAD_DIM

    def gating(j):
        at = pl.ds(pl.multiple_of(j * wide, wide), wide)
        gate = gateb[:, at].astype(F32)
        gsb[:, at] = gainb[:, at] * (gate / (1.0 + jnp.exp(-gate)))

    def collect(h):
        keep(h).wait()
        for k in range(1, n_head):
            scatter(k, h).wait_recv()
        total = sumsq[...]
        for j in range(n_head):
            at = columns(j * heads + h)
            x = rows[j, h].astype(F32)
            total = total + x * x
            gsb[:, at] = x * gsb[:, at]
        sumsq[...] = total

    units = PARTS * heads
    each = chunks // PARTS

    @pl.loop(0, max(units + heads, max(d[0] + d[1] * (heads - 1) for d in DUE) + ROW0_LATER + 1))
    def _(i):
        later = 1 + (i - STATE_DUE[0]) // STATE_DUE[1]

        @pl.when((i >= STATE_DUE[0]) & (later < heads) & (lax.rem(i - STATE_DUE[0], STATE_DUE[1]) == 0))
        def _():
            state(later)
            send_state(later)

        for n, (first, rate) in enumerate(DUE):
            if n == 1:
                first = first + jnp.where(me_z == 0, ROW0_LATER, 0)
            if n == 2:
                lower_first = jnp.where(me_z == 0, DUE[0][0] + 1, DUE[1][0] + 1)
                first = jnp.where(upper, first, lower_first)
            h = (i - first) // rate

            @pl.when((i >= first) & (h < heads) & (lax.rem(i - first, rate) == 0))
            def _(n=n, h=h):
                service(n, h)

        for p in range(PARTS):
            @pl.when((i < units) & (lax.rem(i, PARTS) == p))
            def _(p=p):
                h = i // PARTS
                if p == 0:
                    load_q(h).wait()
                inside(h, range(p * each, (p + 1) * each))

        @pl.when(i == units)
        def _():
            load_gate.wait()
            load_gain.wait()

        @pl.when((i >= units) & (i < units + heads))
        def _():
            gating(i - units)

    @pl.loop(0, heads)
    def _(h):
        collect(h)

    mean_square = jnp.sum(sumsq[...], axis=1, keepdims=True) * (1.0 / (heads * n_head * HEAD_DIM))
    scale = jnp.broadcast_to(lax.rsqrt(mean_square + 1e-06), (tokens_out, HEAD_DIM))
    sumsq[...] = scale

    @pl.loop(0, n_head)
    def _(j):
        for h in range(heads):
            at = columns(j * heads + h)
            out_ref[:, at] = (gsb[:, at] * sumsq[...]).astype(BF16)

    @pl.loop(0, heads)
    def _(h):
        for s in range(steps):
            for j in range(len(plan[s])):
                if s == 0:
                    exchange(s, j, h).wait_send()
                else:
                    @pl.when(sends(s, j))
                    def _(s=s, j=j):
                        exchange(s, j, h).wait_send()

        for k in range(1, n_head):
            scatter(k, h).wait_send()


def per_device(queries, key_vectors, value_vectors, level_weight, gate_values, norm_gain):
    count, features = queries.shape
    heads = features // HEAD_DIM
    n_seq, n_head = lax.axis_size("seq"), lax.axis_size("head")
    levels_out = n_seq.bit_length() - 1
    sends = sum(len(part) for part in PLAN)
    tokens_out, width = gate_values.shape
    chunks = count // CHUNK
    vmem, dma = pltpu.VMEM, pltpu.SemaphoreType.DMA
    return pl.pallas_call(
        functools.partial(kernel, n_seq, n_head),
        out_shape=pltpu.VMEM((tokens_out, width), BF16),
        in_specs=[pl.BlockSpec(memory_space=pl.ANY)] * 6,
        out_specs=pl.BlockSpec(memory_space=pltpu.VMEM),
        scratch_shapes=[
            vmem((heads, count, HEAD_DIM), BF16),
            vmem((heads, count, HEAD_DIM), BF16),
            vmem((heads, count, HEAD_DIM), BF16),
            vmem((count, heads * LEVELS), F32),
            vmem((count, heads * LEVELS), BF16),
            vmem((heads, heads * LEVELS, (chunks.bit_length() - 1 + levels_out) * HEAD_DIM), BF16),
            vmem((tokens_out, width), BF16),
            vmem((1, width), F32),
            vmem((tokens_out, width), F32),
            vmem((CHUNK, CHUNK), jnp.int32),
            vmem((heads, count, HEAD_DIM), F32),
            vmem((heads, count, levels_out * HEAD_DIM), BF16),
            vmem((heads, levels_out * HEAD_DIM, HEAD_DIM), BF16),
            vmem((5, heads, HEAD_DIM, HEAD_DIM), BF16),
            vmem((heads, HEAD_DIM, HEAD_DIM), F32),
            vmem((len(PLAN), heads, HEAD_DIM, HEAD_DIM), BF16),
            vmem((heads, chunks - 1, HEAD_DIM, HEAD_DIM), BF16),
            vmem((heads, count, HEAD_DIM), BF16),
            vmem((n_head, heads, tokens_out, HEAD_DIM), BF16),
            vmem((tokens_out, HEAD_DIM), F32),
            dma((heads,)),
            dma((heads,)),
            dma((heads,)),
            dma,
            dma,
            dma,
            dma((sends, heads)),
            dma((sends, heads)),
            pltpu.SemaphoreType.REGULAR((5,)),
            dma((n_head, heads)),
            dma((n_head, heads)),
            dma((heads,)),
        ],
        compiler_params=pltpu.CompilerParams(
            collective_id=0, has_side_effects=True, vmem_limit_bytes=58 << 20
        ),
    )(queries, key_vectors, value_vectors, level_weight, gate_values, norm_gain[None, :])


def solution(mesh):
    placed = (
        P("seq", "head"),
        P("seq", "head"),
        P("seq", "head"),
        P("seq", "head"),
        P(("seq", "head"), None),
        P(),
    )
    return jax.shard_map(
        per_device, mesh=mesh, in_specs=placed, out_specs=P(("seq", "head"), None), check_vma=False
    )
```

```python
import functools
import jax
import jax.numpy as jnp
from jax import lax
from jax.experimental import pallas as pl
from jax.experimental.pallas import tpu as pltpu
from jax.sharding import PartitionSpec as P

HEAD_DIM = 128
LEVELS = 16
CHUNK = 128
MESH = pl.DeviceIdType.MESH
F32 = jnp.float32
BF16 = jnp.bfloat16


PLAN = ((1, 2, 3), (4, 8, 12), (28, 24))
PARTS = 2
DUE = ((4, 2), (8, 3), (12, 3))
STATE_DUE = (1, 2)
ROW0_LATER = 2
FAR_FIRST = (4, 5, 2, 3, 6, 7, 1)


def kernel(
    n_seq, n_head, q_hbm, k_hbm, v_hbm, w_hbm, gate_hbm, gain_hbm, out_ref,
    qb, kvb, wb, wlow, spread, gateb, gainb, gsb, levb, inner, wq, tiers, xbuf, run, sbuf, loc, att, rows, sumsq,
    q_sem, kv_sem, w_sem, gate_sem, gain_sem,
    xs_sem, xr_sem, ready, ys_sem, yr_sem,
):
    plan = PLAN
    steps = len(plan)
    levels_out = n_seq.bit_length() - 1
    heads = qb.shape[0]
    count = qb.shape[1]
    chunks = count // CHUNK
    chunk_bits = CHUNK.bit_length() - 1
    local_bits = count.bit_length() - 1
    tokens_out = sumsq.shape[0]
    me_seq = lax.axis_index("seq")
    me_head = lax.axis_index("head")

    def columns(h):
        return pl.ds(pl.multiple_of(h * HEAD_DIM, HEAD_DIM), HEAD_DIM)

    def load_k(h):
        return pltpu.make_async_copy(k_hbm.at[:, columns(h)], kvb.at[h, 0], kv_sem.at[jnp.minimum(h, 1)])

    def load_v(h):
        return pltpu.make_async_copy(v_hbm.at[:, columns(h)], kvb.at[h, 1], kv_sem.at[jnp.minimum(h, 1)])

    def load_q(h):
        return pltpu.make_async_copy(q_hbm.at[:, columns(h)], qb.at[h], q_sem)

    def wait_for(ref, sem):
        pltpu.make_async_copy(ref, ref, sem).wait()

    load_w = pltpu.make_async_copy(w_hbm, wb, w_sem)
    load_gate = pltpu.make_async_copy(gate_hbm, gateb, gate_sem)
    load_gain = pltpu.make_async_copy(gain_hbm, gainb, gain_sem)

    def tier_of(m, h):
        return tiers.at[h, m * HEAD_DIM : (m + 1) * HEAD_DIM, :]

    def landing(s, j, h):
        if s == 1:
            return xbuf.at[2 + j, h]
        return tier_of(2 * s, h) if j == 0 or s == 2 else xbuf.at[j - 1, h]

    me_z = lax.shift_right_logical(me_seq, 2)
    in_four = me_z & 3
    upper = me_z >= 4

    def upward(j):
        return (in_four ^ (j + 1)) > in_four

    def downward(j):
        return (me_z ^ (j + 1)) == 0

    def sends(s, j):
        if s == 1:
            return upward(j) | downward(j)
        return (me_z == 0) | (me_z == 3)

    def receives(s, j):
        if s == 1:
            return ((in_four ^ (j + 1)) < in_four) | (me_z == 0)
        near = (me_z == 4) | (me_z == 7) if j == 0 else (me_z == 5) | (me_z == 6)
        return near

    def start_exchange(s, j, h):
        if s == 0:
            exchange(s, j, h).start()
            return

        @pl.when(sends(s, j))
        def _():
            if s == 1:
                @pl.when((h == 0) & upward(j))
                def _():
                    pl.semaphore_wait(ready.at[j], 1)
            else:
                @pl.when(h == 0)
                def _():
                    pl.semaphore_wait(ready.at[3 + j], 1)
            exchange(s, j, h).start()

    def wait_exchange(s, h):
        def wait(pieces):
            wait_for(sbuf.at[0, 0:pieces], xr_sem.at[s, h])

        if s == 0:
            wait(3)
        elif s == 1:
            for pieces in (1, 2, 3):
                @pl.when((in_four == pieces) | ((me_z == 0) & (pieces == 3)))
                def _(pieces=pieces):
                    wait(pieces)
        else:
            @pl.when(upper)
            def _():
                wait(1)

    def row_partner(mask):
        return {"seq": me_seq ^ mask}

    def exchange(s, j, h):
        n = sum(len(p) for p in plan[:s]) + j
        return pltpu.make_async_remote_copy(
            src_ref=sbuf.at[s, h],
            dst_ref=landing(s, j, h),
            send_sem=xs_sem.at[n],
            recv_sem=xr_sem.at[s, h],
            device_id={"seq": me_seq ^ plan[s][j]},
            device_id_type=MESH,
        )

    def tokens_of(j):
        return pl.ds(pl.multiple_of(j * tokens_out, tokens_out), tokens_out)

    def scatter(k, h):
        return pltpu.make_async_remote_copy(
            src_ref=att.at[h, tokens_of(me_head ^ k), :],
            dst_ref=rows.at[me_head, h],
            send_sem=ys_sem,
            recv_sem=yr_sem.at[h],
            device_id={"head": me_head ^ k},
            device_id_type=MESH,
        )

    def keep(h):
        return pltpu.make_async_copy(att.at[h, tokens_of(me_head), :], rows.at[me_head, h], yr_sem.at[h])

    load_k(0).start()
    load_v(0).start()
    barrier = pltpu.get_barrier_semaphore()
    for mask in plan[0]:
        pl.semaphore_signal(barrier, inc=1, device_id=row_partner(mask), device_id_type=MESH)
    for k in range(1, n_head):
        pl.semaphore_signal(barrier, inc=1, device_id={"head": me_head ^ k}, device_id_type=MESH)

    for j, mask in enumerate(plan[1]):
        @pl.when(upward(j))
        def _(mask=mask):
            pl.semaphore_signal(barrier, inc=1, device_id=row_partner(mask), device_id_type=MESH)

    for j, mask in enumerate(plan[2]):
        @pl.when(sends(2, j))
        def _(mask=mask):
            pl.semaphore_signal(barrier, inc=1, device_id=row_partner(mask), device_id_type=MESH)

    @pl.loop(1, heads)
    def _(h):
        load_k(h).start()
        load_v(h).start()

    load_w.start()

    @pl.loop(0, heads)
    def _(h):
        load_q(h).start()

    load_gate.start()
    load_gain.start()

    t_id = lax.broadcasted_iota(jnp.int32, (CHUNK, CHUNK), 0)
    s_id = lax.broadcasted_iota(jnp.int32, (CHUNK, CHUNK), 1)
    mixed = t_id ^ s_id
    level = jnp.zeros((CHUNK, CHUNK), jnp.int32)
    for height in range(chunk_bits):
        level = level + (mixed >= 1 << height).astype(jnp.int32)
    levb[...] = level
    sumsq[...] = jnp.zeros_like(sumsq)

    @pl.loop(0, heads)
    def _(h):
        for s in (1, 2):
            for j in range(len(plan[s])):
                if s == 2 and j == 1:
                    continue
                empty = jnp.logical_not(receives(s, j)) if s == 1 else jnp.logical_not(upper)

                @pl.when(empty)
                def _(s=s, j=j):
                    landing(s, j, h)[...] = jnp.zeros((HEAD_DIM, HEAD_DIM), BF16)

        @pl.when(me_z == 0)
        def _():
            for m in (2, 3):
                tier_of(m, h)[...] = jnp.zeros((HEAD_DIM, HEAD_DIM), BF16)

    @pl.loop(0, heads)
    def _(h):
        row = lax.broadcasted_iota(jnp.int32, (spread.shape[1], HEAD_DIM), 0)
        for n in range(spread.shape[2] // HEAD_DIM):
            here = row == h * LEVELS + chunk_bits + 1 + n
            spread[h, :, n * HEAD_DIM : (n + 1) * HEAD_DIM] = jnp.where(here, F32(1.0), F32(0.0)).astype(BF16)

    def part(h, c):
        at = slice(c * CHUNK, (c + 1) * CHUNK)
        return lax.dot_general(
            kvb[h, 0, at, :], kvb[h, 1, at, :], (((0,), (0,)), ((), ())), preferred_element_type=F32
        )

    def loc_slot(first, half):
        base, size = 0, 1
        while size < half:
            base += chunks // (2 * size)
            size *= 2
        return base + first // (2 * half)

    def span_sum(h, first, size):
        if size == 1:
            return part(h, first)
        half = size // 2
        left = span_sum(h, first, half)
        loc[h, loc_slot(first, half)] = left.astype(BF16)
        return left + span_sum(h, first + half, half)

    def state(h):
        total = span_sum(h, 0, chunks)
        run[h] = total
        sbuf[0, h] = total.astype(BF16)

    def send_state(h):
        for j in range(len(plan[0])):
            start_exchange(0, j, h)

    wait_for(kvb.at[0], kv_sem.at[0])
    state(0)
    pl.semaphore_wait(
        barrier, len(plan[0]) + n_head - 1 + in_four + jnp.where(upper, 1, 0)
    )
    for j, mask in enumerate(plan[1]):
        @pl.when((in_four ^ (j + 1)) < in_four)
        def _(j=j, mask=mask):
            pl.semaphore_signal(
                ready.at[j], inc=1, device_id=row_partner(mask), device_id_type=MESH
            )

    for j, mask in enumerate(plan[2]):
        @pl.when(receives(2, j))
        def _(j=j, mask=mask):
            pl.semaphore_signal(
                ready.at[3 + j], inc=1, device_id=row_partner(mask), device_id_type=MESH
            )

    send_state(0)
    load_w.wait()
    slot = lax.broadcasted_iota(jnp.int32, (1, wb.shape[1]), 1) & (LEVELS - 1)
    taken = jnp.ones((1, wb.shape[1]), F32)
    for m in range(levels_out):
        bit = (lax.shift_right_logical(me_seq, m) & 1).astype(F32)
        taken = jnp.where(slot == local_bits + 1 + m, bit, taken)
    wlow[...] = (wb[...] * taken).astype(BF16)

    def inside(h, which):
        pick = levb[...] + h * LEVELS
        causal = lax.broadcasted_iota(jnp.int32, (CHUNK, CHUNK), 1) <= lax.broadcasted_iota(
            jnp.int32, (CHUNK, CHUNK), 0
        )
        which = list(which)
        base = which[0] * CHUNK
        span = slice(base, base + len(which) * CHUNK)
        inner_bits = chunks.bit_length() - 1

        def weighted_q(n, size, rows_at):
            spread_w = jnp.dot(
                wlow[rows_at, :],
                spread[h, :, n * HEAD_DIM : (n + size) * HEAD_DIM],
                preferred_element_type=F32,
            ).astype(BF16)
            q_rows = qb[h, rows_at, :]
            return [q_rows * spread_w[:, m * HEAD_DIM : (m + 1) * HEAD_DIM] for m in range(size)]

        scores = []
        for c in which:
            at = slice(c * CHUNK, (c + 1) * CHUNK)
            scores.append(
                lax.dot_general(
                    qb[h, at, :], kvb[h, 0, at, :], (((1,), (1,)), ((), ())), preferred_element_type=F32
                )
            )
        for n in range(0, levels_out, 2):
            size = min(2, levels_out - n)
            for m, scaled in enumerate(weighted_q(inner_bits + n, size, span)):
                wq[h, span, (n + m) * HEAD_DIM : (n + m + 1) * HEAD_DIM] = scaled
        lefts = []
        for c, score in zip(which, scores):
            at = slice(c * CHUNK, (c + 1) * CHUNK)
            factor = jnp.take_along_axis(wb[at, :], pick, axis=1)
            left = [jnp.where(causal, score * factor, F32(0.0)).astype(BF16)]
            bits = [n for n in range(inner_bits) if c >> n & 1]
            if bits == [0, 1]:
                left += weighted_q(0, 2, at)
            else:
                for n in bits:
                    left += weighted_q(n, 1, at)
            lefts.append((c, bits, left))
        for c, bits, left in lefts:
            at = slice(c * CHUNK, (c + 1) * CHUNK)
            right = [kvb[h, 1, at, :]] + [
                loc[h, loc_slot((c >> n << n) - (1 << n), 1 << n)] for n in bits
            ]
            inner[h, at, :] = jnp.dot(
                jnp.concatenate(left, axis=1),
                jnp.concatenate(right, axis=0),
                preferred_element_type=F32,
            )

    def service(s, h):
        wait_exchange(s, h)
        if s < steps - 1:
            nearest = landing(s, 0, h)[...]
            pair = landing(s, 1, h)[...].astype(F32) + landing(s, 2, h)[...].astype(F32)
            if s == 0:
                tier_of(1, h)[...] = pair.astype(BF16)
            else:
                @pl.when(me_z != 0)
                def _():
                    tier_of(2, h)[...] = nearest
                    tier_of(3, h)[...] = pair.astype(BF16)

            total = run[h] + nearest.astype(F32) + pair
            run[h] = total
            sbuf[s + 1, h] = total.astype(BF16)
            for j in range(len(plan[s + 1])):
                start_exchange(s + 1, j, h)
            return
        cross = jnp.dot(wq[h], tiers[h], preferred_element_type=F32)
        att[h] = (inner[h] + cross).astype(BF16)
        for k in FAR_FIRST:
            scatter(k, h).start()
        keep(h).start()

    wide = n_head * HEAD_DIM

    def gating(j):
        at = pl.ds(pl.multiple_of(j * wide, wide), wide)
        gate = gateb[:, at].astype(F32)
        gsb[:, at] = gainb[:, at] * (gate / (1.0 + jnp.exp(-gate)))

    def exchanged():
        n = 0
        for s in range(steps):
            for j in range(len(plan[s])):
                if s == 0:
                    wait_for(sbuf.at[s], xs_sem.at[n])
                else:
                    @pl.when(sends(s, j))
                    def _(s=s, n=n):
                        wait_for(sbuf.at[s], xs_sem.at[n])

                n += 1

    def collect(h):
        wait_for(rows.at[0], yr_sem.at[h])
        total = sumsq[...]
        for j in range(n_head):
            at = columns(j * heads + h)
            x = rows[j, h].astype(F32)
            total = total + x * x
            gsb[:, at] = x * gsb[:, at]
        sumsq[...] = total

    units = PARTS * heads
    each = chunks // PARTS

    @pl.loop(0, max(units + heads, max(d[0] + d[1] * (heads - 1) for d in DUE) + ROW0_LATER + 1))
    def _(i):
        later = 1 + (i - STATE_DUE[0]) // STATE_DUE[1]

        @pl.when((i >= STATE_DUE[0]) & (later < heads) & (lax.rem(i - STATE_DUE[0], STATE_DUE[1]) == 0))
        def _():
            @pl.when(later == 1)
            def _():
                wait_for(kvb.at[1:heads], kv_sem.at[1])

            state(later)
            send_state(later)

        for n, (first, rate) in enumerate(DUE):
            if n == 1:
                first = first + jnp.where(me_z == 0, ROW0_LATER, 0)
            if n == 2:
                lower_first = jnp.where(me_z == 0, DUE[0][0] + 1, DUE[1][0] + 1)
                first = jnp.where(upper, first, lower_first)
            h = (i - first) // rate

            @pl.when((i >= first) & (h < heads) & (lax.rem(i - first, rate) == 0))
            def _(n=n, h=h):
                service(n, h)

        for p in range(PARTS):
            @pl.when((i < units) & (lax.rem(i, PARTS) == p))
            def _(p=p):
                h = i // PARTS
                if p == 0:
                    @pl.when(i == 0)
                    def _():
                        wait_for(qb, q_sem)

                inside(h, range(p * each, (p + 1) * each))

        @pl.when(i == units)
        def _():
            load_gate.wait()
            load_gain.wait()

        @pl.when((i >= units) & (i < units + heads))
        def _():
            gating(i - units)

    exchanged()

    @pl.loop(0, heads)
    def _(h):
        collect(h)

    mean_square = jnp.sum(sumsq[...], axis=1, keepdims=True) * (1.0 / (heads * n_head * HEAD_DIM))
    scale = jnp.broadcast_to(lax.rsqrt(mean_square + 1e-06), (tokens_out, HEAD_DIM))
    sumsq[...] = scale

    @pl.loop(0, n_head)
    def _(j):
        for h in range(heads):
            at = columns(j * heads + h)
            out_ref[:, at] = (gsb[:, at] * sumsq[...]).astype(BF16)

    wait_for(att.at[0 : heads * (n_head - 1) // n_head], ys_sem)


def per_device(queries, key_vectors, value_vectors, level_weight, gate_values, norm_gain):
    count, features = queries.shape
    heads = features // HEAD_DIM
    n_seq, n_head = lax.axis_size("seq"), lax.axis_size("head")
    levels_out = n_seq.bit_length() - 1
    sends = sum(len(part) for part in PLAN)
    tokens_out, width = gate_values.shape
    chunks = count // CHUNK
    vmem, dma = pltpu.VMEM, pltpu.SemaphoreType.DMA
    return pl.pallas_call(
        functools.partial(kernel, n_seq, n_head),
        out_shape=pltpu.VMEM((tokens_out, width), BF16),
        in_specs=[pl.BlockSpec(memory_space=pl.ANY)] * 6,
        out_specs=pl.BlockSpec(memory_space=pltpu.VMEM),
        scratch_shapes=[
            vmem((heads, count, HEAD_DIM), BF16),
            vmem((heads, 2, count, HEAD_DIM), BF16),
            vmem((count, heads * LEVELS), F32),
            vmem((count, heads * LEVELS), BF16),
            vmem((heads, heads * LEVELS, (chunks.bit_length() - 1 + levels_out) * HEAD_DIM), BF16),
            vmem((tokens_out, width), BF16),
            vmem((1, width), F32),
            vmem((tokens_out, width), F32),
            vmem((CHUNK, CHUNK), jnp.int32),
            vmem((heads, count, HEAD_DIM), F32),
            vmem((heads, count, levels_out * HEAD_DIM), BF16),
            vmem((heads, levels_out * HEAD_DIM, HEAD_DIM), BF16),
            vmem((5, heads, HEAD_DIM, HEAD_DIM), BF16),
            vmem((heads, HEAD_DIM, HEAD_DIM), F32),
            vmem((len(PLAN), heads, HEAD_DIM, HEAD_DIM), BF16),
            vmem((heads, chunks - 1, HEAD_DIM, HEAD_DIM), BF16),
            vmem((heads, count, HEAD_DIM), BF16),
            vmem((n_head, heads, tokens_out, HEAD_DIM), BF16),
            vmem((tokens_out, HEAD_DIM), F32),
            dma,
            dma((2,)),
            dma,
            dma,
            dma,
            dma((sends,)),
            dma((len(PLAN), heads)),
            pltpu.SemaphoreType.REGULAR((5,)),
            dma,
            dma((heads,)),
        ],
        compiler_params=pltpu.CompilerParams(
            collective_id=0, has_side_effects=True, vmem_limit_bytes=58 << 20
        ),
    )(queries, key_vectors, value_vectors, level_weight, gate_values, norm_gain[None, :])


def solution(mesh):
    placed = (
        P("seq", "head"),
        P("seq", "head"),
        P("seq", "head"),
        P("seq", "head"),
        P(("seq", "head"), None),
        P(),
    )
    return jax.shard_map(
        per_device, mesh=mesh, in_specs=placed, out_specs=P(("seq", "head"), None), check_vma=False
    )
```

```python
import functools
import jax
import jax.numpy as jnp
from jax import lax
from jax.experimental import pallas as pl
from jax.experimental.pallas import tpu as pltpu
from jax.sharding import PartitionSpec as P

HEAD_DIM = 128
LEVELS = 16
CHUNK = 128
MESH = pl.DeviceIdType.MESH
F32 = jnp.float32
BF16 = jnp.bfloat16


PLAN = ((1, 2, 3), (4, 8, 12), (28, 24))
PARTS = 2
DUE = ((4, 2), (8, 3), (11, 3))
STATE_DUE = (1, 2)
ROW0_LATER = 0
FAR_FIRST = (4, 5, 2, 3, 6, 7, 1)


def kernel(
    n_seq, n_head, q_hbm, k_hbm, v_hbm, w_hbm, gate_hbm, gain_hbm, out_ref,
    qb, kvb, wb, wlow, spread, gateb, gainb, gsb, levb, inner, wq, tiers, xbuf, run, sbuf, loc, att, rows, sumsq,
    q_sem, kv_sem, w_sem, gate_sem, gain_sem,
    xs_sem, xr_sem, ready, ys_sem, yr_sem,
):
    plan = PLAN
    steps = len(plan)
    levels_out = n_seq.bit_length() - 1
    heads = qb.shape[0]
    count = qb.shape[1]
    chunks = count // CHUNK
    chunk_bits = CHUNK.bit_length() - 1
    local_bits = count.bit_length() - 1
    tokens_out = sumsq.shape[0]
    me_seq = lax.axis_index("seq")
    me_head = lax.axis_index("head")

    def columns(h):
        return pl.ds(pl.multiple_of(h * HEAD_DIM, HEAD_DIM), HEAD_DIM)

    def load_k(h):
        return pltpu.make_async_copy(k_hbm.at[:, columns(h)], kvb.at[h, 0], kv_sem.at[jnp.minimum(h, 1)])

    def load_v(h):
        return pltpu.make_async_copy(v_hbm.at[:, columns(h)], kvb.at[h, 1], kv_sem.at[jnp.minimum(h, 1)])

    def load_q(h):
        return pltpu.make_async_copy(q_hbm.at[:, columns(h)], qb.at[h], q_sem)

    def wait_for(ref, sem):
        pltpu.make_async_copy(ref, ref, sem).wait()

    load_w = pltpu.make_async_copy(w_hbm, wb, w_sem)
    load_gate = pltpu.make_async_copy(gate_hbm, gateb, gate_sem)
    load_gain = pltpu.make_async_copy(gain_hbm, gainb, gain_sem)

    def tier_of(m, h):
        return tiers.at[h, m * HEAD_DIM : (m + 1) * HEAD_DIM, :]

    def landing(s, j, h):
        if s == 1:
            return xbuf.at[2 + j, h]
        return tier_of(2 * s, h) if j == 0 or s == 2 else xbuf.at[j - 1, h]

    me_z = lax.shift_right_logical(me_seq, 2)
    in_four = me_z & 3
    upper = me_z >= 4

    def upward(j):
        return (in_four ^ (j + 1)) > in_four

    def downward(j):
        return (me_z ^ (j + 1)) == 0

    def sends(s, j):
        if s == 1:
            return upward(j) | downward(j)
        return (me_z == 0) | (me_z == 3)

    def receives(s, j):
        if s == 1:
            return ((in_four ^ (j + 1)) < in_four) | (me_z == 0)
        near = (me_z == 4) | (me_z == 7) if j == 0 else (me_z == 5) | (me_z == 6)
        return near

    def start_exchange(s, j, h):
        if s == 0:
            exchange(s, j, h).start()
            return

        @pl.when(sends(s, j))
        def _():
            if s == 1:
                @pl.when((h == 0) & upward(j))
                def _():
                    pl.semaphore_wait(ready.at[j], 1)
            else:
                @pl.when(h == 0)
                def _():
                    pl.semaphore_wait(ready.at[3 + j], 1)
            exchange(s, j, h).start()

    def wait_exchange(s, h):
        def wait(pieces):
            wait_for(sbuf.at[0, 0:pieces], xr_sem.at[s, h])

        if s == 0:
            wait(3)
        elif s == 1:
            for pieces in (1, 2, 3):
                @pl.when((in_four == pieces) | ((me_z == 0) & (pieces == 3)))
                def _(pieces=pieces):
                    wait(pieces)
        else:
            @pl.when(upper)
            def _():
                wait(1)

    def row_partner(mask):
        return {"seq": me_seq ^ mask}

    def exchange(s, j, h):
        n = sum(len(p) for p in plan[:s]) + j
        return pltpu.make_async_remote_copy(
            src_ref=sbuf.at[s, h],
            dst_ref=landing(s, j, h),
            send_sem=xs_sem.at[n],
            recv_sem=xr_sem.at[s, h],
            device_id={"seq": me_seq ^ plan[s][j]},
            device_id_type=MESH,
        )

    def tokens_of(j):
        return pl.ds(pl.multiple_of(j * tokens_out, tokens_out), tokens_out)

    def scatter(k, h):
        return pltpu.make_async_remote_copy(
            src_ref=att.at[h, tokens_of(me_head ^ k), :],
            dst_ref=rows.at[me_head, h],
            send_sem=ys_sem,
            recv_sem=yr_sem.at[h],
            device_id={"head": me_head ^ k},
            device_id_type=MESH,
        )

    def keep(h):
        return pltpu.make_async_copy(att.at[h, tokens_of(me_head), :], rows.at[me_head, h], yr_sem.at[h])

    load_k(0).start()
    load_v(0).start()
    barrier = pltpu.get_barrier_semaphore()
    for mask in plan[0]:
        pl.semaphore_signal(barrier, inc=1, device_id=row_partner(mask), device_id_type=MESH)
    for k in range(1, n_head):
        pl.semaphore_signal(barrier, inc=1, device_id={"head": me_head ^ k}, device_id_type=MESH)

    for j, mask in enumerate(plan[1]):
        @pl.when(upward(j))
        def _(mask=mask):
            pl.semaphore_signal(barrier, inc=1, device_id=row_partner(mask), device_id_type=MESH)

    for j, mask in enumerate(plan[2]):
        @pl.when(sends(2, j))
        def _(mask=mask):
            pl.semaphore_signal(barrier, inc=1, device_id=row_partner(mask), device_id_type=MESH)

    @pl.loop(1, heads)
    def _(h):
        load_k(h).start()
        load_v(h).start()

    load_w.start()

    @pl.loop(0, heads)
    def _(h):
        load_q(h).start()

    load_gate.start()
    load_gain.start()

    t_id = lax.broadcasted_iota(jnp.int32, (CHUNK, CHUNK), 0)
    s_id = lax.broadcasted_iota(jnp.int32, (CHUNK, CHUNK), 1)
    mixed = t_id ^ s_id
    level = jnp.zeros((CHUNK, CHUNK), jnp.int32)
    for height in range(chunk_bits):
        level = level + (mixed >= 1 << height).astype(jnp.int32)
    levb[...] = level
    sumsq[...] = jnp.zeros_like(sumsq)

    @pl.loop(0, heads)
    def _(h):
        for s in (1, 2):
            for j in range(len(plan[s])):
                if s == 2 and j == 1:
                    continue
                empty = jnp.logical_not(receives(s, j)) if s == 1 else jnp.logical_not(upper)

                @pl.when(empty)
                def _(s=s, j=j):
                    landing(s, j, h)[...] = jnp.zeros((HEAD_DIM, HEAD_DIM), BF16)

        @pl.when(me_z == 0)
        def _():
            for m in (2, 3):
                tier_of(m, h)[...] = jnp.zeros((HEAD_DIM, HEAD_DIM), BF16)

    @pl.loop(0, heads)
    def _(h):
        row = lax.broadcasted_iota(jnp.int32, (spread.shape[1], HEAD_DIM), 0)
        for n in range(spread.shape[2] // HEAD_DIM):
            here = row == h * LEVELS + chunk_bits + 1 + n
            spread[h, :, n * HEAD_DIM : (n + 1) * HEAD_DIM] = jnp.where(here, F32(1.0), F32(0.0)).astype(BF16)

    def part(h, c):
        at = slice(c * CHUNK, (c + 1) * CHUNK)
        return lax.dot_general(
            kvb[h, 0, at, :], kvb[h, 1, at, :], (((0,), (0,)), ((), ())), preferred_element_type=F32
        )

    def loc_slot(first, half):
        base, size = 0, 1
        while size < half:
            base += chunks // (2 * size)
            size *= 2
        return base + first // (2 * half)

    def span_sum(h, first, size):
        if size == 1:
            return part(h, first)
        half = size // 2
        left = span_sum(h, first, half)
        loc[h, loc_slot(first, half)] = left.astype(BF16)
        return left + span_sum(h, first + half, half)

    def state(h):
        total = span_sum(h, 0, chunks)
        run[h] = total
        sbuf[0, h] = total.astype(BF16)

    def send_state(h):
        for j in range(len(plan[0])):
            start_exchange(0, j, h)

    wait_for(kvb.at[0], kv_sem.at[0])
    state(0)
    pl.semaphore_wait(
        barrier, len(plan[0]) + n_head - 1 + in_four + jnp.where(upper, 1, 0)
    )
    for j, mask in enumerate(plan[1]):
        @pl.when((in_four ^ (j + 1)) < in_four)
        def _(j=j, mask=mask):
            pl.semaphore_signal(
                ready.at[j], inc=1, device_id=row_partner(mask), device_id_type=MESH
            )

    for j, mask in enumerate(plan[2]):
        @pl.when(receives(2, j))
        def _(j=j, mask=mask):
            pl.semaphore_signal(
                ready.at[3 + j], inc=1, device_id=row_partner(mask), device_id_type=MESH
            )

    send_state(0)
    load_w.wait()
    slot = lax.broadcasted_iota(jnp.int32, (1, wb.shape[1]), 1) & (LEVELS - 1)
    taken = jnp.ones((1, wb.shape[1]), F32)
    for m in range(levels_out):
        bit = (lax.shift_right_logical(me_seq, m) & 1).astype(F32)
        taken = jnp.where(slot == local_bits + 1 + m, bit, taken)
    wlow[...] = (wb[...] * taken).astype(BF16)

    def inside(h, which):
        pick = levb[...] + h * LEVELS
        causal = lax.broadcasted_iota(jnp.int32, (CHUNK, CHUNK), 1) <= lax.broadcasted_iota(
            jnp.int32, (CHUNK, CHUNK), 0
        )
        which = list(which)
        base = which[0] * CHUNK
        span = slice(base, base + len(which) * CHUNK)
        inner_bits = chunks.bit_length() - 1

        def weighted_q(n, size, rows_at):
            spread_w = jnp.dot(
                wlow[rows_at, :],
                spread[h, :, n * HEAD_DIM : (n + size) * HEAD_DIM],
                preferred_element_type=F32,
            ).astype(BF16)
            q_rows = qb[h, rows_at, :]
            return [q_rows * spread_w[:, m * HEAD_DIM : (m + 1) * HEAD_DIM] for m in range(size)]

        scores = []
        for c in which:
            at = slice(c * CHUNK, (c + 1) * CHUNK)
            scores.append(
                lax.dot_general(
                    qb[h, at, :], kvb[h, 0, at, :], (((1,), (1,)), ((), ())), preferred_element_type=F32
                )
            )
        for n in range(0, levels_out, 2):
            size = min(2, levels_out - n)
            for m, scaled in enumerate(weighted_q(inner_bits + n, size, span)):
                wq[h, span, (n + m) * HEAD_DIM : (n + m + 1) * HEAD_DIM] = scaled
        lefts = []
        for c, score in zip(which, scores):
            at = slice(c * CHUNK, (c + 1) * CHUNK)
            factor = jnp.take_along_axis(wb[at, :], pick, axis=1)
            left = [jnp.where(causal, score * factor, F32(0.0)).astype(BF16)]
            bits = [n for n in range(inner_bits) if c >> n & 1]
            if bits == [0, 1]:
                left += weighted_q(0, 2, at)
            else:
                for n in bits:
                    left += weighted_q(n, 1, at)
            lefts.append((c, bits, left))
        for c, bits, left in lefts:
            at = slice(c * CHUNK, (c + 1) * CHUNK)
            right = [kvb[h, 1, at, :]] + [
                loc[h, loc_slot((c >> n << n) - (1 << n), 1 << n)] for n in bits
            ]
            inner[h, at, :] = jnp.dot(
                jnp.concatenate(left, axis=1),
                jnp.concatenate(right, axis=0),
                preferred_element_type=F32,
            )

    def service(s, h):
        wait_exchange(s, h)
        if s < steps - 1:
            nearest = landing(s, 0, h)[...]
            pair = landing(s, 1, h)[...].astype(F32) + landing(s, 2, h)[...].astype(F32)
            if s == 0:
                tier_of(1, h)[...] = pair.astype(BF16)
            else:
                @pl.when(me_z != 0)
                def _():
                    tier_of(2, h)[...] = nearest
                    tier_of(3, h)[...] = pair.astype(BF16)

            total = run[h] + nearest.astype(F32) + pair
            run[h] = total
            sbuf[s + 1, h] = total.astype(BF16)
            for j in range(len(plan[s + 1])):
                start_exchange(s + 1, j, h)
            return
        cross = jnp.dot(wq[h], tiers[h], preferred_element_type=F32)
        att[h] = (inner[h] + cross).astype(BF16)
        for k in FAR_FIRST:
            scatter(k, h).start()
        keep(h).start()

    wide = n_head * HEAD_DIM

    def gating(j):
        at = pl.ds(pl.multiple_of(j * wide, wide), wide)
        gate = gateb[:, at].astype(F32)
        gsb[:, at] = gainb[:, at] * (gate / (1.0 + jnp.exp(-gate)))

    def exchanged():
        n = 0
        for s in range(steps):
            for j in range(len(plan[s])):
                if s == 0:
                    wait_for(sbuf.at[s], xs_sem.at[n])
                else:
                    @pl.when(sends(s, j))
                    def _(s=s, n=n):
                        wait_for(sbuf.at[s], xs_sem.at[n])

                n += 1

    def collect(h):
        wait_for(rows.at[0], yr_sem.at[h])
        total = sumsq[...]
        for j in range(n_head):
            at = columns(j * heads + h)
            x = rows[j, h].astype(F32)
            total = total + x * x
            gsb[:, at] = x * gsb[:, at]
        sumsq[...] = total

    units = PARTS * heads
    each = chunks // PARTS

    @pl.loop(0, max(units + heads, max(d[0] + d[1] * (heads - 1) for d in DUE) + ROW0_LATER + 1))
    def _(i):
        later = 1 + (i - STATE_DUE[0]) // STATE_DUE[1]

        @pl.when((i >= STATE_DUE[0]) & (later < heads) & (lax.rem(i - STATE_DUE[0], STATE_DUE[1]) == 0))
        def _():
            @pl.when(later == 1)
            def _():
                wait_for(kvb.at[1:heads], kv_sem.at[1])

            state(later)
            send_state(later)

        for n, (first, rate) in enumerate(DUE):
            if n == 1:
                first = first + jnp.where(me_z == 0, ROW0_LATER, 0)
            if n == 2:
                lower_first = jnp.where(me_z == 0, DUE[0][0] + 1, DUE[1][0] + 1)
                first = jnp.where(upper, first, lower_first)
            h = (i - first) // rate

            @pl.when((i >= first) & (h < heads) & (lax.rem(i - first, rate) == 0))
            def _(n=n, h=h):
                service(n, h)

        for p in range(PARTS):
            @pl.when((i < units) & (lax.rem(i, PARTS) == p))
            def _(p=p):
                h = i // PARTS
                if p == 0:
                    @pl.when(i == 0)
                    def _():
                        wait_for(qb, q_sem)

                inside(h, range(p * each, (p + 1) * each))

        @pl.when(i == units)
        def _():
            load_gate.wait()
            load_gain.wait()

        @pl.when((i >= units) & (i < units + heads))
        def _():
            gating(i - units)

    exchanged()

    @pl.loop(0, heads)
    def _(h):
        collect(h)

    mean_square = jnp.sum(sumsq[...], axis=1, keepdims=True) * (1.0 / (heads * n_head * HEAD_DIM))
    scale = lax.rsqrt(mean_square + 1e-06)
    tile = 16
    for r in range(0, tokens_out, tile):
        out_ref[r : r + tile, :] = (gsb[r : r + tile, :] * scale[r : r + tile, :]).astype(BF16)
    wait_for(att.at[0 : heads * (n_head - 1) // n_head], ys_sem)


def per_device(queries, key_vectors, value_vectors, level_weight, gate_values, norm_gain):
    count, features = queries.shape
    heads = features // HEAD_DIM
    n_seq, n_head = lax.axis_size("seq"), lax.axis_size("head")
    levels_out = n_seq.bit_length() - 1
    sends = sum(len(part) for part in PLAN)
    tokens_out, width = gate_values.shape
    chunks = count // CHUNK
    vmem, dma = pltpu.VMEM, pltpu.SemaphoreType.DMA
    return pl.pallas_call(
        functools.partial(kernel, n_seq, n_head),
        out_shape=pltpu.VMEM((tokens_out, width), BF16),
        in_specs=[pl.BlockSpec(memory_space=pl.ANY)] * 6,
        out_specs=pl.BlockSpec(memory_space=pltpu.VMEM),
        scratch_shapes=[
            vmem((heads, count, HEAD_DIM), BF16),
            vmem((heads, 2, count, HEAD_DIM), BF16),
            vmem((count, heads * LEVELS), F32),
            vmem((count, heads * LEVELS), BF16),
            vmem((heads, heads * LEVELS, (chunks.bit_length() - 1 + levels_out) * HEAD_DIM), BF16),
            vmem((tokens_out, width), BF16),
            vmem((1, width), F32),
            vmem((tokens_out, width), F32),
            vmem((CHUNK, CHUNK), jnp.int32),
            vmem((heads, count, HEAD_DIM), F32),
            vmem((heads, count, levels_out * HEAD_DIM), BF16),
            vmem((heads, levels_out * HEAD_DIM, HEAD_DIM), BF16),
            vmem((5, heads, HEAD_DIM, HEAD_DIM), BF16),
            vmem((heads, HEAD_DIM, HEAD_DIM), F32),
            vmem((len(PLAN), heads, HEAD_DIM, HEAD_DIM), BF16),
            vmem((heads, chunks - 1, HEAD_DIM, HEAD_DIM), BF16),
            vmem((heads, count, HEAD_DIM), BF16),
            vmem((n_head, heads, tokens_out, HEAD_DIM), BF16),
            vmem((tokens_out, HEAD_DIM), F32),
            dma,
            dma((2,)),
            dma,
            dma,
            dma,
            dma((sends,)),
            dma((len(PLAN), heads)),
            pltpu.SemaphoreType.REGULAR((5,)),
            dma,
            dma((heads,)),
        ],
        compiler_params=pltpu.CompilerParams(
            collective_id=0, has_side_effects=True, vmem_limit_bytes=58 << 20
        ),
    )(queries, key_vectors, value_vectors, level_weight, gate_values, norm_gain[None, :])


def solution(mesh):
    placed = (
        P("seq", "head"),
        P("seq", "head"),
        P("seq", "head"),
        P("seq", "head"),
        P(("seq", "head"), None),
        P(),
    )
    return jax.shard_map(
        per_device, mesh=mesh, in_specs=placed, out_specs=P(("seq", "head"), None), check_vma=False
    )
```

```python
import functools
import jax
import jax.numpy as jnp
from jax import lax
from jax.experimental import pallas as pl
from jax.experimental.pallas import tpu as pltpu
from jax.sharding import PartitionSpec as P

HEAD_DIM = 128
LEVELS = 16
CHUNK = 128
MESH = pl.DeviceIdType.MESH
F32 = jnp.float32
BF16 = jnp.bfloat16


PLAN = ((1, 2, 3), (4, 8, 12), (28, 24))
PARTS = 2
DUE = ((4, 2), (8, 3), (11, 3))
STATE_DUE = (1, 2)
ROW0_LATER = 0
FAR_FIRST = (4, 5, 2, 3, 6, 7, 1)


def kernel(
    n_seq, n_head, q_hbm, k_hbm, v_hbm, w_hbm, gate_hbm, gain_hbm, out_ref,
    qb, kvb, wb, wlow, spread, gateb, gainb, gsb, levb, inner, wq, tiers, xbuf, run, sbuf, loc, att, rows, sumsq,
    q_sem, kv_sem, w_sem, gate_sem, gain_sem,
    xs_sem, xr_sem, ready, ys_sem, yr_sem,
):
    plan = PLAN
    steps = len(plan)
    levels_out = n_seq.bit_length() - 1
    heads = qb.shape[0]
    count = qb.shape[1]
    chunks = count // CHUNK
    chunk_bits = CHUNK.bit_length() - 1
    local_bits = count.bit_length() - 1
    tokens_out = sumsq.shape[0]
    me_seq = lax.axis_index("seq")
    me_head = lax.axis_index("head")

    def columns(h):
        return pl.ds(pl.multiple_of(h * HEAD_DIM, HEAD_DIM), HEAD_DIM)

    def load_k(h):
        return pltpu.make_async_copy(k_hbm.at[:, columns(h)], kvb.at[h, 0], kv_sem.at[jnp.minimum(h, 1)])

    def load_v(h):
        return pltpu.make_async_copy(v_hbm.at[:, columns(h)], kvb.at[h, 1], kv_sem.at[jnp.minimum(h, 1)])

    def load_q(h):
        return pltpu.make_async_copy(q_hbm.at[:, columns(h)], qb.at[h], q_sem)

    def wait_for(ref, sem):
        pltpu.make_async_copy(ref, ref, sem).wait()

    load_w = pltpu.make_async_copy(w_hbm, wb, w_sem)
    load_gate = pltpu.make_async_copy(gate_hbm, gateb, gate_sem)
    load_gain = pltpu.make_async_copy(gain_hbm, gainb, gain_sem)

    def tier_of(m, h):
        return tiers.at[h, m * HEAD_DIM : (m + 1) * HEAD_DIM, :]

    def landing(s, j, h):
        if s == 1:
            return xbuf.at[2 + j, h]
        return tier_of(2 * s, h) if j == 0 or s == 2 else xbuf.at[j - 1, h]

    me_z = lax.shift_right_logical(me_seq, 2)
    in_four = me_z & 3
    upper = me_z >= 4

    def upward(j):
        return (in_four ^ (j + 1)) > in_four

    def downward(j):
        return (me_z ^ (j + 1)) == 0

    def sends(s, j):
        if s == 1:
            return upward(j) | downward(j)
        return (me_z == 0) | (me_z == 3)

    def receives(s, j):
        if s == 1:
            return ((in_four ^ (j + 1)) < in_four) | (me_z == 0)
        near = (me_z == 4) | (me_z == 7) if j == 0 else (me_z == 5) | (me_z == 6)
        return near

    def start_exchange(s, j, h):
        if s == 0:
            exchange(s, j, h).start()
            return

        @pl.when(sends(s, j))
        def _():
            if s == 1:
                @pl.when((h == 0) & upward(j))
                def _():
                    pl.semaphore_wait(ready.at[j], 1)
            else:
                @pl.when(h == 0)
                def _():
                    pl.semaphore_wait(ready.at[3 + j], 1)
            exchange(s, j, h).start()

    def wait_exchange(s, h):
        def wait(pieces):
            wait_for(sbuf.at[0, 0:pieces], xr_sem.at[s, h])

        if s == 0:
            wait(3)
        elif s == 1:
            for pieces in (1, 2, 3):
                @pl.when((in_four == pieces) | ((me_z == 0) & (pieces == 3)))
                def _(pieces=pieces):
                    wait(pieces)
        else:
            @pl.when(upper)
            def _():
                wait(1)

    def row_partner(mask):
        return {"seq": me_seq ^ mask}

    def exchange(s, j, h):
        n = sum(len(p) for p in plan[:s]) + j
        return pltpu.make_async_remote_copy(
            src_ref=sbuf.at[s, h],
            dst_ref=landing(s, j, h),
            send_sem=xs_sem.at[n],
            recv_sem=xr_sem.at[s, h],
            device_id={"seq": me_seq ^ plan[s][j]},
            device_id_type=MESH,
        )

    def tokens_of(j):
        return pl.ds(pl.multiple_of(j * tokens_out, tokens_out), tokens_out)

    def scatter(k, h):
        return pltpu.make_async_remote_copy(
            src_ref=att.at[h, tokens_of(me_head ^ k), :],
            dst_ref=rows.at[me_head, h],
            send_sem=ys_sem,
            recv_sem=yr_sem.at[h],
            device_id={"head": me_head ^ k},
            device_id_type=MESH,
        )

    def keep(h):
        return pltpu.make_async_copy(att.at[h, tokens_of(me_head), :], rows.at[me_head, h], yr_sem.at[h])

    load_k(0).start()
    load_v(0).start()
    barrier = pltpu.get_barrier_semaphore()
    for mask in plan[0]:
        pl.semaphore_signal(barrier, inc=1, device_id=row_partner(mask), device_id_type=MESH)
    for k in range(1, n_head):
        pl.semaphore_signal(barrier, inc=1, device_id={"head": me_head ^ k}, device_id_type=MESH)

    for j, mask in enumerate(plan[1]):
        @pl.when(upward(j))
        def _(mask=mask):
            pl.semaphore_signal(barrier, inc=1, device_id=row_partner(mask), device_id_type=MESH)

    for j, mask in enumerate(plan[2]):
        @pl.when(sends(2, j))
        def _(mask=mask):
            pl.semaphore_signal(barrier, inc=1, device_id=row_partner(mask), device_id_type=MESH)

    @pl.loop(1, heads)
    def _(h):
        load_k(h).start()
        load_v(h).start()

    load_w.start()

    @pl.loop(0, heads)
    def _(h):
        load_q(h).start()

    load_gate.start()
    load_gain.start()

    t_id = lax.broadcasted_iota(jnp.int32, (CHUNK, CHUNK), 0)
    s_id = lax.broadcasted_iota(jnp.int32, (CHUNK, CHUNK), 1)
    mixed = t_id ^ s_id
    level = jnp.zeros((CHUNK, CHUNK), jnp.int32)
    for height in range(chunk_bits):
        level = level + (mixed >= 1 << height).astype(jnp.int32)
    levb[...] = level
    sumsq[...] = jnp.zeros_like(sumsq)

    @pl.loop(0, heads)
    def _(h):
        for s in (1, 2):
            for j in range(len(plan[s])):
                if s == 2 and j == 1:
                    continue
                empty = jnp.logical_not(receives(s, j)) if s == 1 else jnp.logical_not(upper)

                @pl.when(empty)
                def _(s=s, j=j):
                    landing(s, j, h)[...] = jnp.zeros((HEAD_DIM, HEAD_DIM), BF16)

        @pl.when(me_z == 0)
        def _():
            for m in (2, 3):
                tier_of(m, h)[...] = jnp.zeros((HEAD_DIM, HEAD_DIM), BF16)

    @pl.loop(0, heads)
    def _(h):
        row = lax.broadcasted_iota(jnp.int32, (spread.shape[1], HEAD_DIM), 0)
        for n in range(spread.shape[2] // HEAD_DIM):
            here = row == h * LEVELS + chunk_bits + 1 + n
            spread[h, :, n * HEAD_DIM : (n + 1) * HEAD_DIM] = jnp.where(here, F32(1.0), F32(0.0)).astype(BF16)

    def part(h, c):
        at = slice(c * CHUNK, (c + 1) * CHUNK)
        return lax.dot_general(
            kvb[h, 0, at, :], kvb[h, 1, at, :], (((0,), (0,)), ((), ())), preferred_element_type=F32
        )

    def loc_slot(first, half):
        base, size = 0, 1
        while size < half:
            base += chunks // (2 * size)
            size *= 2
        return base + first // (2 * half)

    def span_sum(h, first, size):
        if size == 1:
            return part(h, first)
        half = size // 2
        left = span_sum(h, first, half)
        loc[h, loc_slot(first, half)] = left.astype(BF16)
        return left + span_sum(h, first + half, half)

    def state(h):
        total = span_sum(h, 0, chunks)
        run[h] = total
        sbuf[0, h] = total.astype(BF16)

    def send_state(h):
        for j in range(len(plan[0])):
            start_exchange(0, j, h)

    wait_for(kvb.at[0], kv_sem.at[0])
    state(0)
    pl.semaphore_wait(
        barrier, len(plan[0]) + n_head - 1 + in_four + jnp.where(upper, 1, 0)
    )
    for j, mask in enumerate(plan[1]):
        @pl.when((in_four ^ (j + 1)) < in_four)
        def _(j=j, mask=mask):
            pl.semaphore_signal(
                ready.at[j], inc=1, device_id=row_partner(mask), device_id_type=MESH
            )

    for j, mask in enumerate(plan[2]):
        @pl.when(receives(2, j))
        def _(j=j, mask=mask):
            pl.semaphore_signal(
                ready.at[3 + j], inc=1, device_id=row_partner(mask), device_id_type=MESH
            )

    send_state(0)
    load_w.wait()
    slot = lax.broadcasted_iota(jnp.int32, (1, wb.shape[1]), 1) & (LEVELS - 1)
    taken = jnp.ones((1, wb.shape[1]), F32)
    for m in range(levels_out):
        bit = (lax.shift_right_logical(me_seq, m) & 1).astype(F32)
        taken = jnp.where(slot == local_bits + 1 + m, bit, taken)
    wlow[...] = (wb[...] * taken).astype(BF16)

    def inside(h, which):
        pick = levb[...] + h * LEVELS
        causal = lax.broadcasted_iota(jnp.int32, (CHUNK, CHUNK), 1) <= lax.broadcasted_iota(
            jnp.int32, (CHUNK, CHUNK), 0
        )
        which = list(which)
        base = which[0] * CHUNK
        span = slice(base, base + len(which) * CHUNK)
        inner_bits = chunks.bit_length() - 1

        def weighted_q(n, size, rows_at):
            spread_w = jnp.dot(
                wlow[rows_at, :],
                spread[h, :, n * HEAD_DIM : (n + size) * HEAD_DIM],
                preferred_element_type=F32,
            ).astype(BF16)
            q_rows = qb[h, rows_at, :]
            return [q_rows * spread_w[:, m * HEAD_DIM : (m + 1) * HEAD_DIM] for m in range(size)]

        scores = []
        for c in which:
            at = slice(c * CHUNK, (c + 1) * CHUNK)
            scores.append(
                lax.dot_general(
                    qb[h, at, :], kvb[h, 0, at, :], (((1,), (1,)), ((), ())), preferred_element_type=F32
                )
            )
        for n in range(0, levels_out, 2):
            size = min(2, levels_out - n)
            for m, scaled in enumerate(weighted_q(inner_bits + n, size, span)):
                wq[h, span, (n + m) * HEAD_DIM : (n + m + 1) * HEAD_DIM] = scaled
        lefts = []
        for c, score in zip(which, scores):
            at = slice(c * CHUNK, (c + 1) * CHUNK)
            factor = jnp.take_along_axis(wb[at, :], pick, axis=1)
            left = [jnp.where(causal, score * factor, F32(0.0)).astype(BF16)]
            bits = [n for n in range(inner_bits) if c >> n & 1]
            if bits == [0, 1]:
                left += weighted_q(0, 2, at)
            else:
                for n in bits:
                    left += weighted_q(n, 1, at)
            lefts.append((c, bits, left))
        for c, bits, left in lefts:
            at = slice(c * CHUNK, (c + 1) * CHUNK)
            right = [kvb[h, 1, at, :]] + [
                loc[h, loc_slot((c >> n << n) - (1 << n), 1 << n)] for n in bits
            ]
            inner[h, at, :] = jnp.dot(
                jnp.concatenate(left, axis=1),
                jnp.concatenate(right, axis=0),
                preferred_element_type=F32,
            )

    def service(s, h):
        wait_exchange(s, h)
        if s < steps - 1:
            nearest = landing(s, 0, h)[...]
            pair = landing(s, 1, h)[...].astype(F32) + landing(s, 2, h)[...].astype(F32)
            if s == 0:
                tier_of(1, h)[...] = pair.astype(BF16)
            else:
                @pl.when(me_z != 0)
                def _():
                    tier_of(2, h)[...] = nearest
                    tier_of(3, h)[...] = pair.astype(BF16)

            total = run[h] + nearest.astype(F32) + pair
            run[h] = total
            sbuf[s + 1, h] = total.astype(BF16)
            for j in range(len(plan[s + 1])):
                start_exchange(s + 1, j, h)
            return
        cross = jnp.dot(wq[h], tiers[h], preferred_element_type=F32)
        att[h] = (inner[h] + cross).astype(BF16)
        for k in FAR_FIRST:
            scatter(k, h).start()
        keep(h).start()

    wide = n_head * HEAD_DIM

    def gating(j):
        at = pl.ds(pl.multiple_of(j * wide, wide), wide)
        gate = gateb[:, at].astype(F32)
        gsb[:, at] = gainb[:, at] * (gate / (1.0 + jnp.exp(-gate)))

    def exchanged():
        n = 0
        for s in range(steps):
            for j in range(len(plan[s])):
                if s == 0:
                    wait_for(sbuf.at[s], xs_sem.at[n])
                else:
                    @pl.when(sends(s, j))
                    def _(s=s, n=n):
                        wait_for(sbuf.at[s], xs_sem.at[n])

                n += 1

    def collect(h):
        wait_for(rows.at[0], yr_sem.at[h])
        total = sumsq[...]
        for j in range(n_head):
            at = columns(j * heads + h)
            x = rows[j, h].astype(F32)
            total = total + x * x
            gsb[:, at] = x * gsb[:, at]
        sumsq[...] = total

    units = PARTS * heads
    each = chunks // PARTS

    @pl.loop(0, max(units + heads, max(d[0] + d[1] * (heads - 1) for d in DUE) + ROW0_LATER + 1))
    def _(i):
        later = 1 + (i - STATE_DUE[0]) // STATE_DUE[1]

        @pl.when((i >= STATE_DUE[0]) & (later < heads) & (lax.rem(i - STATE_DUE[0], STATE_DUE[1]) == 0))
        def _():
            @pl.when(later == 1)
            def _():
                wait_for(kvb.at[1:heads], kv_sem.at[1])

            state(later)
            send_state(later)

        for n in (0, 2, 1):
            first, rate = DUE[n]
            if n == 1:
                first = first + jnp.where(me_z == 0, ROW0_LATER, 0)
            if n == 2:
                lower_first = jnp.where(me_z == 0, DUE[0][0] + 1, DUE[1][0] + 1)
                first = jnp.where(upper, first, lower_first)
            h = (i - first) // rate

            @pl.when((i >= first) & (h < heads) & (lax.rem(i - first, rate) == 0))
            def _(n=n, h=h):
                service(n, h)

        for p in range(PARTS):
            @pl.when((i < units) & (lax.rem(i, PARTS) == p))
            def _(p=p):
                h = i // PARTS
                if p == 0:
                    @pl.when(i == 0)
                    def _():
                        wait_for(qb, q_sem)

                inside(h, range(p * each, (p + 1) * each))

        @pl.when(i == units)
        def _():
            load_gate.wait()
            load_gain.wait()

        @pl.when((i >= units) & (i < units + heads))
        def _():
            gating(i - units)

    exchanged()

    @pl.loop(0, heads)
    def _(h):
        collect(h)

    mean_square = jnp.sum(sumsq[...], axis=1, keepdims=True) * (1.0 / (heads * n_head * HEAD_DIM))
    scale = lax.rsqrt(mean_square + 1e-06)
    tile = 16
    for r in range(0, tokens_out, tile):
        out_ref[r : r + tile, :] = (gsb[r : r + tile, :] * scale[r : r + tile, :]).astype(BF16)
    wait_for(att.at[0 : heads * (n_head - 1) // n_head], ys_sem)


def per_device(queries, key_vectors, value_vectors, level_weight, gate_values, norm_gain):
    count, features = queries.shape
    heads = features // HEAD_DIM
    n_seq, n_head = lax.axis_size("seq"), lax.axis_size("head")
    levels_out = n_seq.bit_length() - 1
    sends = sum(len(part) for part in PLAN)
    tokens_out, width = gate_values.shape
    chunks = count // CHUNK
    vmem, dma = pltpu.VMEM, pltpu.SemaphoreType.DMA
    return pl.pallas_call(
        functools.partial(kernel, n_seq, n_head),
        out_shape=pltpu.VMEM((tokens_out, width), BF16),
        in_specs=[pl.BlockSpec(memory_space=pl.ANY)] * 6,
        out_specs=pl.BlockSpec(memory_space=pltpu.VMEM),
        scratch_shapes=[
            vmem((heads, count, HEAD_DIM), BF16),
            vmem((heads, 2, count, HEAD_DIM), BF16),
            vmem((count, heads * LEVELS), F32),
            vmem((count, heads * LEVELS), BF16),
            vmem((heads, heads * LEVELS, (chunks.bit_length() - 1 + levels_out) * HEAD_DIM), BF16),
            vmem((tokens_out, width), BF16),
            vmem((1, width), F32),
            vmem((tokens_out, width), F32),
            vmem((CHUNK, CHUNK), jnp.int32),
            vmem((heads, count, HEAD_DIM), F32),
            vmem((heads, count, levels_out * HEAD_DIM), BF16),
            vmem((heads, levels_out * HEAD_DIM, HEAD_DIM), BF16),
            vmem((5, heads, HEAD_DIM, HEAD_DIM), BF16),
            vmem((heads, HEAD_DIM, HEAD_DIM), F32),
            vmem((len(PLAN), heads, HEAD_DIM, HEAD_DIM), BF16),
            vmem((heads, chunks - 1, HEAD_DIM, HEAD_DIM), BF16),
            vmem((heads, count, HEAD_DIM), BF16),
            vmem((n_head, heads, tokens_out, HEAD_DIM), BF16),
            vmem((tokens_out, HEAD_DIM), F32),
            dma,
            dma((2,)),
            dma,
            dma,
            dma,
            dma((sends,)),
            dma((len(PLAN), heads)),
            pltpu.SemaphoreType.REGULAR((5,)),
            dma,
            dma((heads,)),
        ],
        compiler_params=pltpu.CompilerParams(
            collective_id=0, has_side_effects=True, vmem_limit_bytes=58 << 20
        ),
    )(queries, key_vectors, value_vectors, level_weight, gate_values, norm_gain[None, :])


def solution(mesh):
    placed = (
        P("seq", "head"),
        P("seq", "head"),
        P("seq", "head"),
        P("seq", "head"),
        P(("seq", "head"), None),
        P(),
    )
    return jax.shard_map(
        per_device, mesh=mesh, in_specs=placed, out_specs=P(("seq", "head"), None), check_vma=False
    )
```
